32 devices in a mesh: segment: 2 (over core), fsdp: 16 (over z, y, x).
Axes of the slice: x: 2, y: 2, z: 4, core: 2. Of those that a mesh axis runs over, the one named last changes fastest.
Arguments:
- inputs: bfloat16 [4, 48, 7, 7, 896], P(None, 'fsdp'), may hold values from -6 to 6
- cotangent: bfloat16 [4, 48, 7, 7, 896], P(None, 'fsdp'), may hold values from -6 to 6
- proj: bfloat16 [2, 896, 896], P('segment', 'fsdp'), may hold values from -0.1875 to 0.1875
- squeeze_weight: bfloat16 [2, 896, 224], P('segment', 'fsdp'), may hold values from -0.75 to 0.75
- excite_weight: bfloat16 [2, 224, 896], P('segment', None, 'fsdp'), may hold values from -0.75 to 0.75
Outputs:
- input_grads: bfloat16 [2, 4, 48, 7, 7, 896], P('segment', None, 'fsdp')
- proj_grads: float32 [2, 896, 896], P('segment', 'fsdp')
- squeeze_grads: float32 [2, 896, 224], P('segment', 'fsdp')
- excite_grads: float32 [2, 224, 896], P('segment', None, 'fsdp')
The draws below stay inside these ranges and needn't reach their ends.
All inputs are finite; a program needn't handle non-finite values.
Results may differ from the reference program's by a relative error of at most 0.0054.
Values may be sent and summed in bfloat16 or wider, within the bound.
A program may use at most 64 MiB of HBM per device.

```python
import jax
import jax.numpy as jnp
from jax import lax

C = 896
SE = 224
H = 7
W = 7
M = 4
B_TOT = 48
SECTIONS = 2
N_SEGMENT = 2


def strengthened(array, own_key, source, target, parts, factor):
    def block_of(position):
        return (jnp.arange(array.shape[position]) // (array.shape[position] // parts)).reshape((-1,) + (1,) * (array.ndim - 1 - position))

    first = jax.random.permutation(own_key, parts)[block_of(target)]
    second = (block_of(target) + parts // 2) % parts
    return jnp.where((block_of(source) == first) | (block_of(source) == second), factor * array, array)


def levels(own_key, dims, split, least, high):
    loudness, own = 1.0, jax.random.fold_in(own_key, 6)
    for axis_at, blocks in split:
        steps = jnp.exp(jax.random.uniform(jax.random.fold_in(own, axis_at), (blocks,), jnp.float32, least / len(split), high / len(split)))
        loudness = loudness * jnp.repeat(steps, dims[axis_at] // blocks).reshape([-1 if axis == axis_at else 1 for axis in range(len(dims))])
    return loudness


def scatter_about(key, dims, deviation, reach, shards=(), held_as=jnp.bfloat16):
    entries = deviation * jax.random.normal(key, dims, jnp.float32)
    if shards:
        entries = entries * levels(key, dims, shards, -0.22, 0.18)
    return jnp.clip(entries, -reach, reach).astype(held_as)


def bell_draw_with(own_key, extent, deviation, limit, split, heavy, kind=jnp.bfloat16):
    entries = deviation * jax.random.normal(own_key, extent, jnp.float32)
    if split:
        entries = entries * levels(own_key, extent, split, -0.22, 0.18)
    return jnp.clip(strengthened(entries, jax.random.fold_in(own_key, 3), *heavy), -limit, limit).astype(kind)


def setup_inputs(seed: int = 0) -> dict:
    arg_keys = jax.random.split(jax.random.key(seed), 6)
    inputs = bell_draw_with(arg_keys[0], (M, B_TOT, H, W, C), 1.0, 6.0, ((1, 16),), (1, 4, 16, 2.0))
    cotangent = scatter_about(arg_keys[1], (M, B_TOT, H, W, C), 1.0, 6.0, ((1, 16),))
    proj = scatter_about(arg_keys[2], (SECTIONS, C, C), C ** -0.5, 0.1875, ((0, 2), (1, 16)))
    squeeze_weight = scatter_about(arg_keys[3], (SECTIONS, C, SE), (C // 16) ** -0.5, 0.75, ((0, 2), (1, 16)))
    excite_weight = scatter_about(arg_keys[4], (SECTIONS, SE, C), (SE // 4) ** -0.5, 0.75, ((0, 2), (2, 16)))
    return {"inputs": inputs, "cotangent": cotangent, "proj": proj, "squeeze_weight": squeeze_weight, "excite_weight": excite_weight}


HIGH = lax.Precision.HIGHEST


def silu_slope(value):
    sig = jax.nn.sigmoid(value)
    return sig * (1.0 + value * (1.0 - sig))


def section_values(hin, weight, squeeze, excite):
    count = hin.shape[0]
    conv = jnp.dot(hin.reshape(-1, C).astype(jnp.float32), weight.astype(jnp.float32), precision=HIGH).reshape(count, H * W, C)
    pooled = jnp.mean(conv, axis=1)
    u_val = jnp.dot(pooled, squeeze.astype(jnp.float32), precision=HIGH)
    z_val = jax.nn.silu(u_val)
    gate = jax.nn.sigmoid(jnp.dot(z_val, excite.astype(jnp.float32), precision=HIGH))
    prod = conv * gate[:, None, :]
    return conv, pooled, u_val, z_val, gate, prod


def reference(inputs, cotangent, proj, squeeze_weight, excite_weight):
    count = M * B_TOT
    hidden = inputs.reshape(count, H * W, C)
    saved = []
    for s in range(N_SEGMENT):
        saved.append(hidden)
        conv, pooled, u_val, z_val, gate, prod = section_values(hidden, proj[s], squeeze_weight[s], excite_weight[s])
        hidden = (hidden.astype(jnp.float32) + jax.nn.silu(prod)).astype(jnp.bfloat16)
    grad_now = cotangent.reshape(count, H * W, C)
    grads_in = [None] * N_SEGMENT
    proj_list = [None] * N_SEGMENT
    sq_list = [None] * N_SEGMENT
    ex_list = [None] * N_SEGMENT
    for s in range(N_SEGMENT - 1, -1, -1):
        hin = saved[s]
        conv, pooled, u_val, z_val, gate, prod = section_values(hin, proj[s], squeeze_weight[s], excite_weight[s])
        dyf = grad_now.astype(jnp.float32)
        dprod = dyf * silu_slope(prod)
        dgate = jnp.sum(dprod * conv, axis=1)
        dv_val = dgate * gate * (1.0 - gate)
        ex_list[s] = jnp.dot(z_val.T, dv_val, precision=HIGH)
        du_val = jnp.dot(dv_val, excite_weight[s].astype(jnp.float32).T, precision=HIGH) * silu_slope(u_val)
        sq_list[s] = jnp.dot(pooled.T, du_val, precision=HIGH)
        dpooled = jnp.dot(du_val, squeeze_weight[s].astype(jnp.float32).T, precision=HIGH)
        dconv = (dprod * gate[:, None, :] + dpooled[:, None, :] / (H * W)).astype(jnp.bfloat16)
        flat_d = dconv.reshape(-1, C).astype(jnp.float32)
        back = jnp.dot(flat_d, proj[s].astype(jnp.float32).T, precision=HIGH)
        grad_now = (dyf.reshape(-1, C) + back).astype(jnp.bfloat16).reshape(count, H * W, C)
        proj_list[s] = jnp.dot(hin.reshape(-1, C).astype(jnp.float32).T, flat_d, precision=HIGH)
        grads_in[s] = grad_now.reshape(M, B_TOT, H, W, C)
    return (jnp.stack(grads_in), jnp.stack(proj_list), jnp.stack(sq_list), jnp.stack(ex_list))
```

```python
import functools

import jax
import jax.numpy as jnp
from jax import lax
from jax.experimental import pallas as pl
from jax.experimental.pallas import tpu as pltpu
from jax.sharding import PartitionSpec as P

HIGH = lax.Precision.HIGHEST


def shifted(block, axis, distance):
    devices = range(lax.axis_size(axis))
    route = [(i - distance, i) for i in devices if i - distance in devices]
    return lax.ppermute(block, axis, route)


def silu_slope(value):
    sig = jax.nn.sigmoid(value)
    return sig * (1.0 + value * (1.0 - sig))


def gate_values(conv, squeeze, excite):
    pooled = jnp.mean(conv, axis=1)
    u_val = jnp.dot(pooled, squeeze.astype(jnp.float32), precision=HIGH)
    gate = jax.nn.sigmoid(jnp.dot(jax.nn.silu(u_val), excite.astype(jnp.float32), precision=HIGH))
    return (pooled, u_val, gate)


def run_forward(hin, weight, squeeze, excite):
    count, chans = (hin.shape[0], hin.shape[3])
    conv = jnp.dot(hin.reshape(-1, chans), weight, preferred_element_type=jnp.float32).reshape(
        count, -1, chans
    )
    pooled, u_val, gate = gate_values(conv, squeeze, excite)
    prod = conv * gate[:, None, :]
    out = (hin.reshape(count, -1, chans).astype(jnp.float32) + jax.nn.silu(prod)).astype(
        jnp.bfloat16
    )
    return (out.reshape(hin.shape), conv, pooled, u_val)


def run_backward(grad_in, hin, weight, squeeze, excite, conv, u_val):
    count, chans = (grad_in.shape[0], grad_in.shape[3])
    positions = conv.shape[1]
    z_val = jax.nn.silu(u_val)
    gate = jax.nn.sigmoid(jnp.dot(z_val, excite.astype(jnp.float32), precision=HIGH))
    prod = conv * gate[:, None, :]
    dyf = grad_in.reshape(count, positions, chans).astype(jnp.float32)
    dprod = dyf * silu_slope(prod)
    dgate = jnp.sum(dprod * conv, axis=1)
    dv_val = dgate * gate * (1.0 - gate)
    du_val = jnp.dot(dv_val, excite.astype(jnp.float32).T, precision=HIGH) * silu_slope(u_val)
    dpooled = jnp.dot(du_val, squeeze.astype(jnp.float32).T, precision=HIGH)
    dconv = (dprod * gate[:, None, :] + dpooled[:, None, :] / positions).astype(jnp.bfloat16)
    flat_d = dconv.reshape(-1, chans)
    back = lax.dot_general(
        flat_d, weight, (((1,), (1,)), ((), ())), preferred_element_type=jnp.float32
    )
    grad_out = (dyf.reshape(-1, chans) + back).astype(jnp.bfloat16).reshape(grad_in.shape)
    w_term = lax.dot_general(
        hin.reshape(-1, chans), flat_d, (((0,), (0,)), ((), ())), preferred_element_type=jnp.float32
    )
    return (grad_out, w_term, du_val, dv_val)


def store(buffer, value, index, valid):
    old = lax.dynamic_index_in_dim(buffer, index, 0, keepdims=False)
    return lax.dynamic_update_index_in_dim(buffer, jnp.where(valid, value, old), index, 0)


def fetch(buffer, index):
    return lax.dynamic_index_in_dim(buffer, index, 0, keepdims=False)


def body(inputs, cotangent, proj, squeeze_weight, excite_weight):
    segments = lax.axis_size("segment")
    here = lax.axis_index("segment")
    micro, batch, height, width, chans = inputs.shape
    inner = squeeze_weight.shape[2]
    positions = height * width
    full_proj, full_sq, full_ex = (
        lax.all_gather(proj, "fsdp", axis=1, tiled=True),
        lax.all_gather(squeeze_weight, "fsdp", axis=1, tiled=True),
        lax.all_gather(excite_weight, "fsdp", axis=2, tiled=True),
    )
    weight, squeeze, excite = (full_proj[0], full_sq[0], full_ex[0])
    act_shape = (micro, batch, height, width, chans)

    def forward_step(tick, incoming, fbufs):
        hin_buf, conv_buf, pool_buf, u_buf = fbufs
        index = tick - here
        valid = (index >= 0) & (index < micro)
        slot = jnp.clip(index, 0, micro - 1)
        feed = jnp.where(here == 0, fetch(inputs, slot), incoming)

        def forward_active(hin):
            return run_forward(hin, weight, squeeze, excite)

        def forward_resting(hin):
            return (
                jnp.zeros(hin.shape, jnp.bfloat16),
                jnp.zeros((batch, positions, chans), jnp.float32),
                jnp.zeros((batch, chans), jnp.float32),
                jnp.zeros((batch, inner), jnp.float32),
            )

        out, conv, pooled, u_val = lax.cond(valid, forward_active, forward_resting, feed)
        fbufs = (
            store(hin_buf, feed, slot, valid),
            store(conv_buf, conv, slot, valid),
            store(pool_buf, pooled, slot, valid),
            store(u_buf, u_val, slot, valid),
        )
        sent = shifted(out, "segment", 1)
        return (sent, fbufs)

    def backward_step(tick, offset, incoming, fbufs, bbufs):
        hin_buf, conv_buf, pool_buf, u_buf = fbufs
        grad_buf, du_buf, dv_buf, w_acc = bbufs
        index = tick - offset
        valid = (index >= 0) & (index < micro)
        slot = jnp.clip(index, 0, micro - 1)
        feed = jnp.where(here == segments - 1, fetch(cotangent, slot), incoming)
        hin = fetch(hin_buf, slot)
        conv = fetch(conv_buf, slot)
        pooled = fetch(pool_buf, slot)
        u_val = fetch(u_buf, slot)

        def backward_active(grad_in):
            return run_backward(grad_in, hin, weight, squeeze, excite, conv, u_val)

        def backward_resting(grad_in):
            return (
                jnp.zeros(grad_in.shape, jnp.bfloat16),
                jnp.zeros((chans, chans), jnp.float32),
                jnp.zeros((batch, inner), jnp.float32),
                jnp.zeros((batch, chans), jnp.float32),
            )

        grad_out, w_term, du_val, dv_val = lax.cond(valid, backward_active, backward_resting, feed)
        bbufs = (
            store(grad_buf, grad_out, slot, valid),
            store(du_buf, du_val, slot, valid),
            store(dv_buf, dv_val, slot, valid),
            w_acc + w_term,
        )
        sent = shifted(grad_out, "segment", -1)
        return (sent, bbufs)

    fstart = (
        jnp.zeros(act_shape, jnp.bfloat16),
        jnp.zeros((micro, batch, positions, chans), jnp.float32),
        jnp.zeros((micro, batch, chans), jnp.float32),
        jnp.zeros((micro, batch, inner), jnp.float32),
    )
    bstart = (
        jnp.zeros(act_shape, jnp.bfloat16),
        jnp.zeros((micro, batch, inner), jnp.float32),
        jnp.zeros((micro, batch, chans), jnp.float32),
        jnp.zeros((chans, chans), jnp.float32),
    )
    empty = jnp.zeros(act_shape[1:], jnp.bfloat16)
    ticks = micro + segments - 1

    def forward_tick(tick, carry):
        return forward_step(tick, carry[0], carry[1])

    _, fbufs = lax.fori_loop(0, ticks, forward_tick, (empty, fstart))

    def backward_tick(tick, carry):
        return backward_step(tick, segments - 1 - here, carry[0], fbufs, carry[1])

    _, bbufs = lax.fori_loop(0, ticks, backward_tick, (empty, bstart))
    grad_buf, du_buf, dv_buf, w_acc = bbufs
    pool_buf, u_buf = (fbufs[2], fbufs[3])
    proj_grads = lax.psum_scatter(w_acc[None], "fsdp", scatter_dimension=1, tiled=True)
    pool_flat = pool_buf.reshape(micro * batch, chans)
    z_flat = jax.nn.silu(u_buf.reshape(micro * batch, inner))
    du_flat = du_buf.reshape(micro * batch, inner)
    dv_flat = dv_buf.reshape(micro * batch, chans)
    sq_local = jnp.dot(pool_flat.T, du_flat, precision=HIGH)
    ex_local = jnp.dot(z_flat.T, dv_flat, precision=HIGH)
    sq_total, ex_total = lax.psum((sq_local, ex_local), "fsdp")
    share = chans // lax.axis_size("fsdp")
    begin = lax.axis_index("fsdp") * share
    sq_grads = lax.dynamic_slice_in_dim(sq_total, begin, share, 0)[None]
    ex_grads = lax.dynamic_slice_in_dim(ex_total, begin, share, 1)[None]
    return (grad_buf[None], proj_grads, sq_grads, ex_grads)


MESH = pl.DeviceIdType.MESH
F32 = jnp.float32
BF16 = jnp.bfloat16
CHUNKS = 2
PIX = 64
GRP = 16


def sigm(v):
    return 0.5 * jnp.tanh(0.5 * v) + 0.5


def halves(a):
    hi = a.astype(BF16).astype(F32)
    return hi, a - hi


def dot_split(a, b, transposed):
    rows = a.shape[0]
    hi, lo = halves(a)
    dims = (((1,), (1 if transposed else 0,)), ((), ()))
    out = lax.dot_general(
        jnp.concatenate([hi, lo], 0).astype(BF16), b, dims, preferred_element_type=F32
    )
    return out[:rows] + out[rows:]


def outer_split(a, b):
    ah, al = halves(a)
    bh, bl = halves(b)
    left = jnp.concatenate([ah, ah, al], 0).astype(BF16)
    right = jnp.concatenate([bh, bl, bh], 0).astype(BF16)
    return lax.dot_general(left, right, (((0,), (0,)), ((), ())), preferred_element_type=F32)


def fused_kernel(
    size, x_ref, cot_ref, a_ref, b_ref, gout_ref, pg_ref, sg_ref, eg_ref,
    ga, gb, w_ref, sq_ref, ex_ref, hbuf, hnext, dybuf, conv, dpb, dconv,
    pooled, u_s, gate_s, dgate, dpool, z_s, du_s, dv_s, wg,
    sa, sb, rxa, rxb, rya, ryb, rza, rzb,
    ag_send, ag_recv, rs_send, rs_recv, relay_send, relay_recv,
):
    zdim, share, images = size
    chans = w_ref.shape[0]
    cut = a_ref.shape[1] - sq_ref.shape[1]
    seg = lax.axis_index("segment")
    me = lax.axis_index("fsdp")
    z, y, x = me // 4, (me // 2) % 2, me % 2
    core = (1 - seg, me)

    def place(zz, yy, xx):
        return (seg, zz * 4 + yy * 2 + xx)

    barrier = pltpu.get_barrier_semaphore()
    pl.semaphore_signal(barrier, inc=1, device_id=core, device_id_type=MESH)
    pl.semaphore_signal(barrier, inc=1, device_id=place(z, y, 1 - x), device_id_type=MESH)
    pl.semaphore_signal(barrier, inc=1, device_id=place(z, 1 - y, x), device_id_type=MESH)
    for step in range(1, zdim):
        pl.semaphore_signal(
            barrier, inc=1, device_id=place((z + step) % zdim, y, x), device_id_type=MESH
        )
    pl.semaphore_wait(barrier, 2 + zdim)

    parts = ((0, ga, a_ref), (1, gb, b_ref))

    def flip(part, minor):
        if (part == 0) != minor:
            return z, 1 - y, x
        return z, y, 1 - x

    def ag_copy(part, buf, block, kind, target, src=None):
        return pltpu.make_async_remote_copy(
            src_ref=buf.at[block] if src is None else src,
            dst_ref=buf.at[block],
            send_sem=ag_send.at[part, kind, block],
            recv_sem=ag_recv.at[part, block],
            device_id=target,
            device_id_type=MESH,
        )

    def column(zz):
        return zz * 4 + y * 2 + x

    def first_block(part, zz):
        return zz * 4 + ((1 - y) * 2 + x if part == 0 else y * 2 + (1 - x))

    def second_block(part, zz):
        return zz * 4 + (y * 2 + (1 - x) if part == 0 else (1 - y) * 2 + x)

    def far_block(zz):
        return zz * 4 + (1 - y) * 2 + (1 - x)

    up, down = z + 1, z - 1

    def spread(part, buf, zz, src=None):
        block = column(zz)
        ag_copy(part, buf, block, 2, place(*flip(part, False)), src).start()
        ag_copy(part, buf, block, 3, place(*flip(part, True)), src).start()

    for part, buf, own in parts:
        block = column(z)

        @pl.when(up < zdim)
        def _(part=part, buf=buf, own=own, block=block):
            ag_copy(part, buf, block, 0, place(up, y, x), own).start()

        @pl.when(down >= 0)
        def _(part=part, buf=buf, own=own, block=block):
            ag_copy(part, buf, block, 1, place(down, y, x), own).start()

        spread(part, buf, z, own)
    for _, buf, own in parts:
        buf[me] = own[...]

    @pl.when(seg == 0)
    def _():
        hbuf[...] = x_ref[...]

    @pl.when(seg == 1)
    def _():
        dybuf[...] = cot_ref[...]

    pooled[...] = jnp.zeros_like(pooled)
    dgate[...] = jnp.zeros_like(dgate)

    def relay_first(part, buf, zz):
        block = first_block(part, zz)
        ag_copy(part, buf, block, 3, place(*flip(part, True))).wait_recv()
        ag_copy(part, buf, block, 3, place(*flip(part, True))).start()

    for part, buf, own in parts:
        relay_first(part, buf, z)
    for dist in range(1, zdim):
        for part, buf, own in parts:

            @pl.when(z - dist >= 0)
            def _(part=part, buf=buf, dist=dist):
                block = column(z - dist)
                ag_copy(part, buf, block, 0, core).wait_recv()

                @pl.when(up < zdim)
                def _():
                    ag_copy(part, buf, block, 0, place(up, y, x)).start()

                spread(part, buf, z - dist)

            @pl.when(z + dist < zdim)
            def _(part=part, buf=buf, dist=dist):
                block = column(z + dist)
                ag_copy(part, buf, block, 1, core).wait_recv()

                @pl.when(down >= 0)
                def _():
                    ag_copy(part, buf, block, 1, place(down, y, x)).start()

                spread(part, buf, z + dist)

        for part, buf, own in parts:

            @pl.when(z - dist >= 0)
            def _(part=part, buf=buf, dist=dist):
                relay_first(part, buf, z - dist)

            @pl.when(z + dist < zdim)
            def _(part=part, buf=buf, dist=dist):
                relay_first(part, buf, z + dist)

    for part, buf, own in parts:
        for zz in range(zdim):
            ag_copy(part, buf, second_block(part, zz), 3, core).wait_recv()
            ag_copy(part, buf, far_block(zz), 3, core).wait_recv()

    def pack(k, _):
        rows = pl.ds(pl.multiple_of(k * 2 * share, 2 * share), 2 * share)
        pa = jnp.concatenate([ga[2 * k].astype(F32), ga[2 * k + 1].astype(F32)], 0).astype(BF16)
        pb = jnp.concatenate([gb[2 * k].astype(F32), gb[2 * k + 1].astype(F32)], 0).astype(BF16)
        w_ref[rows, :cut] = pa[:, :cut]
        sq_ref[rows, :] = pa[:, cut:]
        w_ref[rows, cut:] = pb[:, : chans - cut]
        ex_ref[rows, :] = pb[:, chans - cut :]
        return 0

    lax.fori_loop(0, 2 * zdim, pack, 0)

    def relay(src, dst, way, j):
        return pltpu.make_async_remote_copy(
            src_ref=src.at[j],
            dst_ref=dst.at[j],
            send_sem=relay_send.at[way, j],
            recv_sem=relay_recv.at[way, j],
            device_id=core,
            device_id_type=MESH,
        )

    def rows_of(i, g):
        return pl.ds(pl.multiple_of(i * PIX + g * GRP, GRP), GRP)

    groups = PIX // GRP

    def forward(j, _):
        @pl.when(seg == 1)
        def _():
            relay(hnext, hbuf, 0, j).wait_recv()

        conv[j] = jnp.dot(hbuf[j], w_ref[...], preferred_element_type=F32)

        def pool(i, _):
            acc = conv[j, rows_of(i, 0), :]
            for g in range(1, groups):
                acc = acc + conv[j, rows_of(i, g), :]
            pooled[j, pl.ds(i, 1), :] = jnp.sum(acc, axis=0, keepdims=True) * (1.0 / 49.0)
            return 0

        lax.fori_loop(0, images, pool, 0)
        u = dot_split(pooled[j], sq_ref[...], False)
        u_s[j] = u
        zv = u * sigm(u)
        z_s[j] = zv
        gate_s[j] = sigm(dot_split(zv, ex_ref[...], True))

        @pl.when(seg == 0)
        def _():
            def emit(i, _):
                g_row = gate_s[j, pl.ds(i, 1), :]
                for g in range(groups):
                    p = conv[j, rows_of(i, g), :] * g_row
                    h = hbuf[j, rows_of(i, g), :].astype(F32)
                    hnext[j, rows_of(i, g), :] = (h + p * sigm(p)).astype(BF16)
                return 0

            lax.fori_loop(0, images, emit, 0)
            relay(hnext, hbuf, 0, j).start()

        return 0

    lax.fori_loop(0, CHUNKS, forward, 0)

    def backward(j, _):
        @pl.when(seg == 0)
        def _():
            relay(gout_ref, dybuf, 1, j).wait_recv()

        def slope(i, _):
            g_row = gate_s[j, pl.ds(i, 1), :]
            total = jnp.zeros((GRP, chans), F32)
            for g in range(groups):
                c = conv[j, rows_of(i, g), :]
                p = c * g_row
                sig = sigm(p)
                dp = dybuf[j, rows_of(i, g), :].astype(F32) * (sig * (1.0 + p * (1.0 - sig)))
                total = total + dp * c
                dpb[rows_of(i, g), :] = dp
            dgate[pl.ds(i, 1), :] = jnp.sum(total, axis=0, keepdims=True)
            return 0

        lax.fori_loop(0, images, slope, 0)
        gate = gate_s[j]
        dv = dgate[...] * gate * (1.0 - gate)
        dv_s[j] = dv
        u = u_s[j]
        sig = sigm(u)
        du = dot_split(dv, ex_ref[...], False) * (sig * (1.0 + u * (1.0 - sig)))
        du_s[j] = du
        dpool[...] = dot_split(du, sq_ref[...], True) * (1.0 / 49.0)
        spot = lax.broadcasted_iota(jnp.int32, (GRP, chans), 0)

        def finish(i, _):
            g_row = gate_s[j, pl.ds(i, 1), :]
            d_row = dpool[pl.ds(i, 1), :]
            for g in range(groups):
                at = spot + g * GRP
                keep = (at % 8 < 7) & (at < 56)
                val = dpb[rows_of(i, g), :] * g_row + d_row
                dconv[j, rows_of(i, g), :] = jnp.where(keep, val, 0.0).astype(BF16)
            return 0

        lax.fori_loop(0, images, finish, 0)
        back = lax.dot_general(
            dconv[j], w_ref[...], (((1,), (1,)), ((), ())), preferred_element_type=F32
        )
        gout_ref[j] = (dybuf[j].astype(F32) + back).astype(BF16)

        @pl.when(seg == 1)
        def _():
            relay(gout_ref, dybuf, 1, j).start()

        return 0

    lax.fori_loop(0, CHUNKS, backward, 0)

    total_rows = CHUNKS * images * PIX
    flat_d = dconv[...].reshape(total_rows, chans)

    def grad_rows(k, _):
        cols = pl.ds(pl.multiple_of(k * 128, 128), 128)
        h = hbuf[:, :, cols].reshape(total_rows, 128)
        wg[pl.ds(pl.multiple_of(k * 128, 128), 128), :chans] = lax.dot_general(
            h, flat_d, (((0,), (0,)), ((), ())), preferred_element_type=F32
        )
        return 0

    lax.fori_loop(0, chans // 128, grad_rows, 0)
    inner = sq_ref.shape[1]
    small = CHUNKS * pooled.shape[1]
    wg[:, chans : chans + inner] = outer_split(
        pooled[...].reshape(small, chans), du_s[...].reshape(small, inner)
    )
    wg[:, chans + inner :] = outer_split(
        dv_s[...].reshape(small, chans), z_s[...].reshape(small, inner)
    )

    def term(part, block):
        rows = pl.ds(pl.multiple_of(block * share, 8), share)
        if part == 0:
            return wg[rows, :cut], wg[rows, chans : chans + inner]
        return wg[rows, cut:chans], wg[rows, chans + inner :]

    rs = ((0, sa, rxa, rya, rza), (1, sb, rxb, ryb, rzb))

    def joined(part, block):
        return jnp.concatenate(term(part, block), axis=1)

    def rs_copy(part, src, dst, index, target):
        return pltpu.make_async_remote_copy(
            src_ref=src,
            dst_ref=dst,
            send_sem=rs_send.at[part, index],
            recv_sem=rs_recv.at[part, index],
            device_id=target,
            device_id_type=MESH,
        )

    def z_at(k):
        return (z + 1 + k) % zdim

    def one(part, stage, r1, k, side):
        zz = z_at(k)
        block = far_block(zz) if side == 0 else second_block(part, zz)
        return block, rs_copy(
            part, stage.at[block], r1.at[2 * k + side], 2 * k + side, place(*flip(part, True))
        )

    def two(part, stage, r2, k):
        block = first_block(part, z_at(k))
        return block, rs_copy(
            part, stage.at[block], r2.at[k], 2 * zdim + k, place(*flip(part, False))
        )

    def three(part, stage, r3, k):
        block = column(z_at(k))
        return block, rs_copy(
            part, stage.at[block], r3.at[k], 3 * zdim + k, place(z_at(k), y, x)
        )

    for k in range(zdim):
        for side in range(2):
            for part, stage, r1, r2, r3 in rs:
                block, copy = one(part, stage, r1, k, side)
                stage[block] = joined(part, block).astype(BF16)
                copy.start()
    for k in range(zdim):
        for part, stage, r1, r2, r3 in rs:
            one(part, stage, r1, k, 0)[1].wait_recv()
            block, copy = two(part, stage, r2, k)
            stage[block] = (joined(part, block) + r1[2 * k].astype(F32)).astype(BF16)
            copy.start()
    for k in range(zdim):
        for part, stage, r1, r2, r3 in rs:
            one(part, stage, r1, k, 1)[1].wait_recv()
            two(part, stage, r2, k)[1].wait_recv()
            if k < zdim - 1:
                block, copy = three(part, stage, r3, k)
                value = joined(part, block) + r1[2 * k + 1].astype(F32) + r2[k].astype(F32)
                stage[block] = value.astype(BF16)
                copy.start()
    last = zdim - 1
    for part, stage, r1, r2, r3 in rs:
        value = joined(part, me) + r1[2 * last + 1].astype(F32) + r2[last].astype(F32)
        for k in range(zdim - 1):
            three(part, stage, r3, k)[1].wait_recv()
            value = value + r3[k].astype(F32)
        if part == 0:
            pg_ref[:, :cut] = value[:, :cut]
            sg_ref[...] = value[:, cut:]
        else:
            pg_ref[:, cut:] = value[:, : chans - cut]
            eg_ref[...] = value[:, chans - cut :]

    for part, stage, r1, r2, r3 in rs:
        for k in range(zdim):
            one(part, stage, r1, k, 0)[1].wait_send()
            one(part, stage, r1, k, 1)[1].wait_send()
            two(part, stage, r2, k)[1].wait_send()
            if k < zdim - 1:
                three(part, stage, r3, k)[1].wait_send()
    for part, buf, own in parts:
        for zz in range(zdim):
            ag_copy(part, buf, column(zz), 2, core).wait_send()
            ag_copy(part, buf, column(zz), 3, core).wait_send()
            ag_copy(part, buf, first_block(part, zz), 3, core).wait_send()

            @pl.when((zz <= z) & (up < zdim))
            def _(part=part, buf=buf, zz=zz):
                ag_copy(part, buf, column(zz), 0, core).wait_send()

            @pl.when((zz >= z) & (down >= 0))
            def _(part=part, buf=buf, zz=zz):
                ag_copy(part, buf, column(zz), 1, core).wait_send()

    for j in range(CHUNKS):

        @pl.when(seg == 0)
        def _(j=j):
            relay(hnext, hbuf, 0, j).wait_send()

        @pl.when(seg == 1)
        def _(j=j):
            relay(gout_ref, dybuf, 1, j).wait_send()


def fused_body(inputs, cotangent, proj, squeeze_weight, excite_weight):
    fsdp = lax.axis_size("fsdp")
    micro, batch, height, width, chans = inputs.shape
    share, inner = squeeze_weight.shape[1:]
    zdim = fsdp // 4
    images = micro * batch // CHUNKS
    rows = images * PIX
    wide = -(-inner // 128) * 128
    cut = (chans // 128 + 1) // 2 * 128
    narrow = -(-images // 8) * 8

    def padded(arr):
        arr = jnp.pad(arr, ((0, 0), (0, 0), (0, 8 - height), (0, 8 - width), (0, 0)))
        return arr.reshape(CHUNKS, rows, chans)

    def widened(arr):
        return jnp.pad(arr, ((0, 0), (0, wide - inner)))

    part_a = jnp.concatenate([proj[0, :, :cut], widened(squeeze_weight[0])], 1)
    part_b = jnp.concatenate([proj[0, :, cut:], widened(excite_weight[0].T)], 1)
    ca, cb = part_a.shape[1], part_b.shape[1]
    vm = pl.BlockSpec(memory_space=pltpu.VMEM)
    v = pltpu.VMEM
    dma = pltpu.SemaphoreType.DMA
    act = v((CHUNKS, rows, chans), BF16)

    def small(cols):
        return v((CHUNKS, narrow, cols), F32)

    gout, pg, sg, eg = pl.pallas_call(
        functools.partial(fused_kernel, (zdim, share, images)),
        out_shape=(
            jax.ShapeDtypeStruct((CHUNKS, rows, chans), BF16),
            jax.ShapeDtypeStruct((share, chans), F32),
            jax.ShapeDtypeStruct((share, wide), F32),
            jax.ShapeDtypeStruct((share, wide), F32),
        ),
        in_specs=[vm] * 4,
        out_specs=(vm,) * 4,
        scratch_shapes=[
            v((fsdp, share, ca), BF16), v((fsdp, share, cb), BF16),
            v((chans, chans), BF16), v((chans, wide), BF16), v((chans, wide), BF16),
            act, act, act,
            v((CHUNKS, rows, chans), F32), v((rows, chans), F32), act,
            small(chans), small(wide), small(chans),
            v((narrow, chans), F32), v((narrow, chans), F32),
            small(wide), small(wide), small(chans),
            v((chans, chans + 2 * wide), F32),
            v((fsdp, share, ca), BF16), v((fsdp, share, cb), BF16),
            v((2 * zdim, share, ca), BF16), v((2 * zdim, share, cb), BF16),
            v((zdim, share, ca), BF16), v((zdim, share, cb), BF16),
            v((zdim, share, ca), BF16), v((zdim, share, cb), BF16),
            dma((2, 4, fsdp)), dma((2, fsdp)),
            dma((2, 4 * zdim)), dma((2, 4 * zdim)),
            dma((2, CHUNKS)), dma((2, CHUNKS)),
        ],
        compiler_params=pltpu.CompilerParams(collective_id=0, has_side_effects=True),
    )(padded(inputs), padded(cotangent), part_a, part_b)
    grads = gout.reshape(micro, batch, 8, 8, chans)[:, :, :height, :width]
    return grads[None], pg[None], sg[None, :, :inner], eg[:, :inner].T[None]


def suits(mesh):
    return mesh.shape["segment"] == 2 and mesh.shape["fsdp"] == 16


def solution(mesh):
    placed = (
        P(None, "fsdp", None, None, None),
        P(None, "fsdp", None, None, None),
        P("segment", "fsdp", None),
        P("segment", "fsdp", None),
        P("segment", None, "fsdp"),
    )
    return jax.shard_map(
        fused_body if suits(mesh) else body,
        mesh=mesh,
        in_specs=placed,
        out_specs=(
            P("segment", None, "fsdp", None, None, None),
            P("segment", "fsdp", None),
            P("segment", "fsdp", None),
            P("segment", None, "fsdp"),
        ),
        check_vma=False,
    )
```

```python
import functools

import jax
import jax.numpy as jnp
from jax import lax
from jax.experimental import pallas as pl
from jax.experimental.pallas import tpu as pltpu
from jax.sharding import PartitionSpec as P

HIGH = lax.Precision.HIGHEST


def shifted(block, axis, distance):
    devices = range(lax.axis_size(axis))
    route = [(i - distance, i) for i in devices if i - distance in devices]
    return lax.ppermute(block, axis, route)


def silu_slope(value):
    sig = jax.nn.sigmoid(value)
    return sig * (1.0 + value * (1.0 - sig))


def gate_values(conv, squeeze, excite):
    pooled = jnp.mean(conv, axis=1)
    u_val = jnp.dot(pooled, squeeze.astype(jnp.float32), precision=HIGH)
    gate = jax.nn.sigmoid(jnp.dot(jax.nn.silu(u_val), excite.astype(jnp.float32), precision=HIGH))
    return (pooled, u_val, gate)


def run_forward(hin, weight, squeeze, excite):
    count, chans = (hin.shape[0], hin.shape[3])
    conv = jnp.dot(hin.reshape(-1, chans), weight, preferred_element_type=jnp.float32).reshape(
        count, -1, chans
    )
    pooled, u_val, gate = gate_values(conv, squeeze, excite)
    prod = conv * gate[:, None, :]
    out = (hin.reshape(count, -1, chans).astype(jnp.float32) + jax.nn.silu(prod)).astype(
        jnp.bfloat16
    )
    return (out.reshape(hin.shape), conv, pooled, u_val)


def run_backward(grad_in, hin, weight, squeeze, excite, conv, u_val):
    count, chans = (grad_in.shape[0], grad_in.shape[3])
    positions = conv.shape[1]
    z_val = jax.nn.silu(u_val)
    gate = jax.nn.sigmoid(jnp.dot(z_val, excite.astype(jnp.float32), precision=HIGH))
    prod = conv * gate[:, None, :]
    dyf = grad_in.reshape(count, positions, chans).astype(jnp.float32)
    dprod = dyf * silu_slope(prod)
    dgate = jnp.sum(dprod * conv, axis=1)
    dv_val = dgate * gate * (1.0 - gate)
    du_val = jnp.dot(dv_val, excite.astype(jnp.float32).T, precision=HIGH) * silu_slope(u_val)
    dpooled = jnp.dot(du_val, squeeze.astype(jnp.float32).T, precision=HIGH)
    dconv = (dprod * gate[:, None, :] + dpooled[:, None, :] / positions).astype(jnp.bfloat16)
    flat_d = dconv.reshape(-1, chans)
    back = lax.dot_general(
        flat_d, weight, (((1,), (1,)), ((), ())), preferred_element_type=jnp.float32
    )
    grad_out = (dyf.reshape(-1, chans) + back).astype(jnp.bfloat16).reshape(grad_in.shape)
    w_term = lax.dot_general(
        hin.reshape(-1, chans), flat_d, (((0,), (0,)), ((), ())), preferred_element_type=jnp.float32
    )
    return (grad_out, w_term, du_val, dv_val)


def store(buffer, value, index, valid):
    old = lax.dynamic_index_in_dim(buffer, index, 0, keepdims=False)
    return lax.dynamic_update_index_in_dim(buffer, jnp.where(valid, value, old), index, 0)


def fetch(buffer, index):
    return lax.dynamic_index_in_dim(buffer, index, 0, keepdims=False)


def body(inputs, cotangent, proj, squeeze_weight, excite_weight):
    segments = lax.axis_size("segment")
    here = lax.axis_index("segment")
    micro, batch, height, width, chans = inputs.shape
    inner = squeeze_weight.shape[2]
    positions = height * width
    full_proj, full_sq, full_ex = (
        lax.all_gather(proj, "fsdp", axis=1, tiled=True),
        lax.all_gather(squeeze_weight, "fsdp", axis=1, tiled=True),
        lax.all_gather(excite_weight, "fsdp", axis=2, tiled=True),
    )
    weight, squeeze, excite = (full_proj[0], full_sq[0], full_ex[0])
    act_shape = (micro, batch, height, width, chans)

    def forward_step(tick, incoming, fbufs):
        hin_buf, conv_buf, pool_buf, u_buf = fbufs
        index = tick - here
        valid = (index >= 0) & (index < micro)
        slot = jnp.clip(index, 0, micro - 1)
        feed = jnp.where(here == 0, fetch(inputs, slot), incoming)

        def forward_active(hin):
            return run_forward(hin, weight, squeeze, excite)

        def forward_resting(hin):
            return (
                jnp.zeros(hin.shape, jnp.bfloat16),
                jnp.zeros((batch, positions, chans), jnp.float32),
                jnp.zeros((batch, chans), jnp.float32),
                jnp.zeros((batch, inner), jnp.float32),
            )

        out, conv, pooled, u_val = lax.cond(valid, forward_active, forward_resting, feed)
        fbufs = (
            store(hin_buf, feed, slot, valid),
            store(conv_buf, conv, slot, valid),
            store(pool_buf, pooled, slot, valid),
            store(u_buf, u_val, slot, valid),
        )
        sent = shifted(out, "segment", 1)
        return (sent, fbufs)

    def backward_step(tick, offset, incoming, fbufs, bbufs):
        hin_buf, conv_buf, pool_buf, u_buf = fbufs
        grad_buf, du_buf, dv_buf, w_acc = bbufs
        index = tick - offset
        valid = (index >= 0) & (index < micro)
        slot = jnp.clip(index, 0, micro - 1)
        feed = jnp.where(here == segments - 1, fetch(cotangent, slot), incoming)
        hin = fetch(hin_buf, slot)
        conv = fetch(conv_buf, slot)
        pooled = fetch(pool_buf, slot)
        u_val = fetch(u_buf, slot)

        def backward_active(grad_in):
            return run_backward(grad_in, hin, weight, squeeze, excite, conv, u_val)

        def backward_resting(grad_in):
            return (
                jnp.zeros(grad_in.shape, jnp.bfloat16),
                jnp.zeros((chans, chans), jnp.float32),
                jnp.zeros((batch, inner), jnp.float32),
                jnp.zeros((batch, chans), jnp.float32),
            )

        grad_out, w_term, du_val, dv_val = lax.cond(valid, backward_active, backward_resting, feed)
        bbufs = (
            store(grad_buf, grad_out, slot, valid),
            store(du_buf, du_val, slot, valid),
            store(dv_buf, dv_val, slot, valid),
            w_acc + w_term,
        )
        sent = shifted(grad_out, "segment", -1)
        return (sent, bbufs)

    fstart = (
        jnp.zeros(act_shape, jnp.bfloat16),
        jnp.zeros((micro, batch, positions, chans), jnp.float32),
        jnp.zeros((micro, batch, chans), jnp.float32),
        jnp.zeros((micro, batch, inner), jnp.float32),
    )
    bstart = (
        jnp.zeros(act_shape, jnp.bfloat16),
        jnp.zeros((micro, batch, inner), jnp.float32),
        jnp.zeros((micro, batch, chans), jnp.float32),
        jnp.zeros((chans, chans), jnp.float32),
    )
    empty = jnp.zeros(act_shape[1:], jnp.bfloat16)
    ticks = micro + segments - 1

    def forward_tick(tick, carry):
        return forward_step(tick, carry[0], carry[1])

    _, fbufs = lax.fori_loop(0, ticks, forward_tick, (empty, fstart))

    def backward_tick(tick, carry):
        return backward_step(tick, segments - 1 - here, carry[0], fbufs, carry[1])

    _, bbufs = lax.fori_loop(0, ticks, backward_tick, (empty, bstart))
    grad_buf, du_buf, dv_buf, w_acc = bbufs
    pool_buf, u_buf = (fbufs[2], fbufs[3])
    proj_grads = lax.psum_scatter(w_acc[None], "fsdp", scatter_dimension=1, tiled=True)
    pool_flat = pool_buf.reshape(micro * batch, chans)
    z_flat = jax.nn.silu(u_buf.reshape(micro * batch, inner))
    du_flat = du_buf.reshape(micro * batch, inner)
    dv_flat = dv_buf.reshape(micro * batch, chans)
    sq_local = jnp.dot(pool_flat.T, du_flat, precision=HIGH)
    ex_local = jnp.dot(z_flat.T, dv_flat, precision=HIGH)
    sq_total, ex_total = lax.psum((sq_local, ex_local), "fsdp")
    share = chans // lax.axis_size("fsdp")
    begin = lax.axis_index("fsdp") * share
    sq_grads = lax.dynamic_slice_in_dim(sq_total, begin, share, 0)[None]
    ex_grads = lax.dynamic_slice_in_dim(ex_total, begin, share, 1)[None]
    return (grad_buf[None], proj_grads, sq_grads, ex_grads)


MESH = pl.DeviceIdType.MESH
F32 = jnp.float32
BF16 = jnp.bfloat16
GRP = 16


def sigm(v):
    return 0.5 * jnp.tanh(0.5 * v) + 0.5


def halves(a):
    hi = a.astype(BF16).astype(F32)
    return hi, a - hi


def dot_split(a, b, transposed):
    rows = a.shape[0]
    hi, lo = halves(a)
    dims = (((1,), (1 if transposed else 0,)), ((), ()))
    out = lax.dot_general(
        jnp.concatenate([hi, lo], 0).astype(BF16), b, dims, preferred_element_type=F32
    )
    return out[:rows] + out[rows:]


def outer_split(a, b):
    fill = -a.shape[0] % GRP
    a = jnp.concatenate([a, jnp.zeros((fill, a.shape[1]), F32)], 0)
    b = jnp.concatenate([b, jnp.zeros((fill, b.shape[1]), F32)], 0)
    ah, al = halves(a)
    bh, bl = halves(b)
    left = jnp.concatenate([ah, ah, al], 0).astype(BF16)
    right = jnp.concatenate([bh, bl, bh], 0).astype(BF16)
    return lax.dot_general(left, right, (((0,), (0,)), ((), ())), preferred_element_type=F32)


def fused_kernel(
    size, x_ref, cot_ref, a_ref, b_ref, gout_ref, pg_ref, sg_ref, eg_ref,
    ga, gb, w_ref, sq_ref, ex_ref, hbuf, hnext, dybuf, conv, dpb, dconv,
    pooled, u_s, gate_s, dpool, z_s, du_s, dv_s, wg,
    sa, sb, rxa, rxb, rya, ryb, rza, rzb,
    ag_send, ag_recv, rs_send, rs_recv, relay_send, relay_recv,
):
    zdim, share = size
    chunks, positions, micro, _ = x_ref.shape
    rows = hbuf.shape[1]
    packs = rows // GRP
    chans = w_ref.shape[0]
    cut = a_ref.shape[1] - sq_ref.shape[1]
    seg = lax.axis_index("segment")
    me = lax.axis_index("fsdp")
    z, y, x = me // 4, (me // 2) % 2, me % 2
    core = (1 - seg, me)

    def place(zz, yy, xx):
        return (seg, zz * 4 + yy * 2 + xx)

    barrier = pltpu.get_barrier_semaphore()
    pl.semaphore_signal(barrier, inc=1, device_id=core, device_id_type=MESH)
    pl.semaphore_signal(barrier, inc=1, device_id=place(z, y, 1 - x), device_id_type=MESH)
    pl.semaphore_signal(barrier, inc=1, device_id=place(z, 1 - y, x), device_id_type=MESH)
    for step in range(1, zdim):
        pl.semaphore_signal(
            barrier, inc=1, device_id=place((z + step) % zdim, y, x), device_id_type=MESH
        )
    pl.semaphore_wait(barrier, 2 + zdim)

    parts = ((0, ga, a_ref), (1, gb, b_ref))

    def flip(part, minor):
        if (part == 0) != minor:
            return z, 1 - y, x
        return z, y, 1 - x

    def ag_copy(part, buf, block, kind, target, src=None):
        return pltpu.make_async_remote_copy(
            src_ref=buf.at[block] if src is None else src,
            dst_ref=buf.at[block],
            send_sem=ag_send.at[part, kind, block],
            recv_sem=ag_recv.at[part, block],
            device_id=target,
            device_id_type=MESH,
        )

    def column(zz):
        return zz * 4 + y * 2 + x

    def first_block(part, zz):
        return zz * 4 + ((1 - y) * 2 + x if part == 0 else y * 2 + (1 - x))

    def second_block(part, zz):
        return zz * 4 + (y * 2 + (1 - x) if part == 0 else (1 - y) * 2 + x)

    def far_block(zz):
        return zz * 4 + (1 - y) * 2 + (1 - x)

    up, down = z + 1, z - 1

    def spread(part, buf, zz, src=None):
        block = column(zz)
        ag_copy(part, buf, block, 2, place(*flip(part, False)), src).start()
        ag_copy(part, buf, block, 3, place(*flip(part, True)), src).start()

    for part, buf, own in parts:
        block = column(z)

        @pl.when(up < zdim)
        def _(part=part, buf=buf, own=own, block=block):
            ag_copy(part, buf, block, 0, place(up, y, x), own).start()

        @pl.when(down >= 0)
        def _(part=part, buf=buf, own=own, block=block):
            ag_copy(part, buf, block, 1, place(down, y, x), own).start()

        spread(part, buf, z, own)
    for _, buf, own in parts:
        buf[me] = own[...]

    def rows_of(q):
        return pl.ds(pl.multiple_of(q * GRP, GRP), GRP)

    def load(src, dst):
        step = GRP // micro

        def one_chunk(j, _):
            def group(q, _):
                four = [src[j, q * step + t].astype(F32) for t in range(step)]
                dst[j, rows_of(q), :] = jnp.concatenate(four, 0).astype(BF16)
                return 0

            lax.fori_loop(0, positions // step, group, 0)
            for q in range(positions // step, packs):
                four = [
                    src[j, q * step + t].astype(F32)
                    if q * step + t < positions
                    else jnp.zeros((micro, chans), F32)
                    for t in range(step)
                ]
                dst[j, q * GRP : (q + 1) * GRP, :] = jnp.concatenate(four, 0).astype(BF16)
            return 0

        lax.fori_loop(0, chunks, one_chunk, 0)

    @pl.when(seg == 0)
    def _():
        load(x_ref, hbuf)

    @pl.when(seg == 1)
    def _():
        load(cot_ref, dybuf)


    def relay_first(part, buf, zz):
        block = first_block(part, zz)
        ag_copy(part, buf, block, 3, place(*flip(part, True))).wait_recv()
        ag_copy(part, buf, block, 3, place(*flip(part, True))).start()

    for part, buf, own in parts:
        relay_first(part, buf, z)
    for dist in range(1, zdim):
        for part, buf, own in parts:

            @pl.when(z - dist >= 0)
            def _(part=part, buf=buf, dist=dist):
                block = column(z - dist)
                ag_copy(part, buf, block, 0, core).wait_recv()

                @pl.when(up < zdim)
                def _():
                    ag_copy(part, buf, block, 0, place(up, y, x)).start()

                spread(part, buf, z - dist)

            @pl.when(z + dist < zdim)
            def _(part=part, buf=buf, dist=dist):
                block = column(z + dist)
                ag_copy(part, buf, block, 1, core).wait_recv()

                @pl.when(down >= 0)
                def _():
                    ag_copy(part, buf, block, 1, place(down, y, x)).start()

                spread(part, buf, z + dist)

        for part, buf, own in parts:

            @pl.when(z - dist >= 0)
            def _(part=part, buf=buf, dist=dist):
                relay_first(part, buf, z - dist)

            @pl.when(z + dist < zdim)
            def _(part=part, buf=buf, dist=dist):
                relay_first(part, buf, z + dist)

    for part, buf, own in parts:
        for zz in range(zdim):
            ag_copy(part, buf, second_block(part, zz), 3, core).wait_recv()
            ag_copy(part, buf, far_block(zz), 3, core).wait_recv()

    def pack(k, _):
        at = pl.ds(pl.multiple_of(k * 2 * share, 2 * share), 2 * share)
        pa = jnp.concatenate([ga[2 * k].astype(F32), ga[2 * k + 1].astype(F32)], 0).astype(BF16)
        pb = jnp.concatenate([gb[2 * k].astype(F32), gb[2 * k + 1].astype(F32)], 0).astype(BF16)
        w_ref[at, :cut] = pa[:, :cut]
        sq_ref[at, :] = pa[:, cut:]
        w_ref[at, cut:] = pb[:, : chans - cut]
        ex_ref[at, :] = pb[:, chans - cut :]
        return 0

    lax.fori_loop(0, 2 * zdim, pack, 0)

    def relay(src, dst, way, j):
        return pltpu.make_async_remote_copy(
            src_ref=src.at[j],
            dst_ref=dst.at[j],
            send_sem=relay_send.at[way, j],
            recv_sem=relay_recv.at[way, j],
            device_id=core,
            device_id_type=MESH,
        )

    real = lax.broadcasted_iota(jnp.int32, (8, chans), 0) < micro

    def fold(acc):
        both = acc[:8] + acc[8:]
        return jnp.where(real, both + pltpu.roll(both, micro, 0), 0.0)

    def twice(v):
        v = jnp.where(real, v, 0.0)
        return v + pltpu.roll(v, micro, 0)

    def forward(j, _):
        @pl.when(seg == 1)
        def _():
            relay(hnext, hbuf, 0, j).wait_recv()

        conv[j] = jnp.dot(hbuf[j], w_ref[...], preferred_element_type=F32)

        def pool(q, acc):
            return acc + conv[j, rows_of(q), :]

        total = lax.fori_loop(0, packs, pool, jnp.zeros((GRP, chans), F32))
        mean = fold(total) * (1.0 / positions)
        pooled[j] = mean
        u = dot_split(mean, sq_ref[...], False)
        u_s[j] = u
        zv = u * sigm(u)
        z_s[j] = zv
        gate = twice(sigm(dot_split(zv, ex_ref[...], True)))
        gate_s[j] = jnp.concatenate([gate, gate], 0)

        @pl.when(seg == 0)
        def _():
            def emit(q, _):
                p = conv[j, rows_of(q), :] * gate_s[j]
                h = hbuf[j, rows_of(q), :].astype(F32)
                hnext[j, rows_of(q), :] = (h + p * sigm(p)).astype(BF16)
                return 0

            lax.fori_loop(0, packs, emit, 0)
            relay(hnext, hbuf, 0, j).start()

        return 0

    lax.fori_loop(0, chunks, forward, 0)

    def backward(j, _):
        @pl.when(seg == 0)
        def _():
            relay(gout_ref, dybuf, 1, j).wait_recv()

        def slope(q, total):
            c = conv[j, rows_of(q), :]
            p = c * gate_s[j]
            sig = sigm(p)
            dp = dybuf[j, rows_of(q), :].astype(F32) * (sig * (1.0 + p * (1.0 - sig)))
            dpb[rows_of(q), :] = dp
            return total + dp * c

        total = lax.fori_loop(0, packs, slope, jnp.zeros((GRP, chans), F32))
        gate = gate_s[j, :8]
        dv = fold(total) * gate * (1.0 - gate)
        dv_s[j] = dv
        u = u_s[j]
        sig = sigm(u)
        du = dot_split(dv, ex_ref[...], False) * (sig * (1.0 + u * (1.0 - sig)))
        du_s[j] = du
        spread_d = twice(dot_split(du, sq_ref[...], True)) * (1.0 / positions)
        dpool[...] = jnp.concatenate([spread_d, spread_d], 0)
        spot = lax.broadcasted_iota(jnp.int32, (GRP, chans), 0)

        def finish(q, _):
            val = dpb[rows_of(q), :] * gate_s[j] + dpool[...]
            keep = spot + q * GRP < positions * micro
            dconv[j, rows_of(q), :] = jnp.where(keep, val, 0.0).astype(BF16)
            return 0

        lax.fori_loop(0, packs, finish, 0)
        back = lax.dot_general(
            dconv[j], w_ref[...], (((1,), (1,)), ((), ())), preferred_element_type=F32
        )
        gout_ref[j] = (dybuf[j].astype(F32) + back).astype(BF16)

        @pl.when(seg == 1)
        def _():
            relay(gout_ref, dybuf, 1, j).start()

        return 0

    lax.fori_loop(0, chunks, backward, 0)

    total_rows = chunks * rows
    flat_d = dconv[...].reshape(total_rows, chans)

    def grad_rows(k, _):
        cols = pl.ds(pl.multiple_of(k * 128, 128), 128)
        h = hbuf[:, :, cols].reshape(total_rows, 128)
        wg[pl.ds(pl.multiple_of(k * 128, 128), 128), :chans] = lax.dot_general(
            h, flat_d, (((0,), (0,)), ((), ())), preferred_element_type=F32
        )
        return 0

    lax.fori_loop(0, chans // 128, grad_rows, 0)
    inner = sq_ref.shape[1]
    small = chunks * pooled.shape[1]
    wg[:, chans : chans + inner] = outer_split(
        pooled[...].reshape(small, chans), du_s[...].reshape(small, inner)
    )
    wg[:, chans + inner :] = outer_split(
        dv_s[...].reshape(small, chans), z_s[...].reshape(small, inner)
    )

    def term(part, block):
        rows = pl.ds(pl.multiple_of(block * share, 8), share)
        if part == 0:
            return wg[rows, :cut], wg[rows, chans : chans + inner]
        return wg[rows, cut:chans], wg[rows, chans + inner :]

    rs = ((0, sa, rxa, rya, rza), (1, sb, rxb, ryb, rzb))

    def joined(part, block):
        return jnp.concatenate(term(part, block), axis=1)

    def rs_copy(part, src, dst, index, target):
        return pltpu.make_async_remote_copy(
            src_ref=src,
            dst_ref=dst,
            send_sem=rs_send.at[part, index],
            recv_sem=rs_recv.at[part, index],
            device_id=target,
            device_id_type=MESH,
        )

    def z_at(k):
        return (z + 1 + k) % zdim

    def one(part, stage, r1, k, side):
        zz = z_at(k)
        block = far_block(zz) if side == 0 else second_block(part, zz)
        return block, rs_copy(
            part, stage.at[block], r1.at[2 * k + side], 2 * k + side, place(*flip(part, True))
        )

    def two(part, stage, r2, k):
        block = first_block(part, z_at(k))
        return block, rs_copy(
            part, stage.at[block], r2.at[k], 2 * zdim + k, place(*flip(part, False))
        )

    def three(part, stage, r3, k):
        block = column(z_at(k))
        return block, rs_copy(
            part, stage.at[block], r3.at[k], 3 * zdim + k, place(z_at(k), y, x)
        )

    for k in range(zdim):
        for side in range(2):
            for part, stage, r1, r2, r3 in rs:
                block, copy = one(part, stage, r1, k, side)
                stage[block] = joined(part, block).astype(BF16)
                copy.start()
    for k in range(zdim):
        for part, stage, r1, r2, r3 in rs:
            one(part, stage, r1, k, 0)[1].wait_recv()
            block, copy = two(part, stage, r2, k)
            stage[block] = (joined(part, block) + r1[2 * k].astype(F32)).astype(BF16)
            copy.start()
    for k in range(zdim):
        for part, stage, r1, r2, r3 in rs:
            one(part, stage, r1, k, 1)[1].wait_recv()
            two(part, stage, r2, k)[1].wait_recv()
            if k < zdim - 1:
                block, copy = three(part, stage, r3, k)
                value = joined(part, block) + r1[2 * k + 1].astype(F32) + r2[k].astype(F32)
                stage[block] = value.astype(BF16)
                copy.start()
    last = zdim - 1
    for part, stage, r1, r2, r3 in rs:
        value = joined(part, me) + r1[2 * last + 1].astype(F32) + r2[last].astype(F32)
        for k in range(zdim - 1):
            three(part, stage, r3, k)[1].wait_recv()
            value = value + r3[k].astype(F32)
        if part == 0:
            pg_ref[:, :cut] = value[:, :cut]
            sg_ref[...] = value[:, cut:]
        else:
            pg_ref[:, cut:] = value[:, : chans - cut]
            eg_ref[...] = value[:, chans - cut :]

    for part, stage, r1, r2, r3 in rs:
        for k in range(zdim):
            one(part, stage, r1, k, 0)[1].wait_send()
            one(part, stage, r1, k, 1)[1].wait_send()
            two(part, stage, r2, k)[1].wait_send()
            if k < zdim - 1:
                three(part, stage, r3, k)[1].wait_send()
    for part, buf, own in parts:
        for zz in range(zdim):
            ag_copy(part, buf, column(zz), 2, core).wait_send()
            ag_copy(part, buf, column(zz), 3, core).wait_send()
            ag_copy(part, buf, first_block(part, zz), 3, core).wait_send()

            @pl.when((zz <= z) & (up < zdim))
            def _(part=part, buf=buf, zz=zz):
                ag_copy(part, buf, column(zz), 0, core).wait_send()

            @pl.when((zz >= z) & (down >= 0))
            def _(part=part, buf=buf, zz=zz):
                ag_copy(part, buf, column(zz), 1, core).wait_send()

    for j in range(chunks):

        @pl.when(seg == 0)
        def _(j=j):
            relay(hnext, hbuf, 0, j).wait_send()

        @pl.when(seg == 1)
        def _(j=j):
            relay(gout_ref, dybuf, 1, j).wait_send()


def fused_body(inputs, cotangent, proj, squeeze_weight, excite_weight):
    fsdp = lax.axis_size("fsdp")
    micro, batch, height, width, chans = inputs.shape
    share, inner = squeeze_weight.shape[1:]
    zdim = fsdp // 4
    positions = height * width
    rows = -(-positions * micro // GRP) * GRP
    wide = -(-inner // 128) * 128
    cut = (chans // 128 + 1) // 2 * 128

    def by_image(arr):
        return arr.transpose(1, 2, 3, 0, 4).reshape(batch, positions, micro, chans)

    def widened(arr):
        return jnp.pad(arr, ((0, 0), (0, wide - inner)))

    part_a = jnp.concatenate([proj[0, :, :cut], widened(squeeze_weight[0])], 1)
    part_b = jnp.concatenate([proj[0, :, cut:], widened(excite_weight[0].T)], 1)
    ca, cb = part_a.shape[1], part_b.shape[1]
    vm = pl.BlockSpec(memory_space=pltpu.VMEM)
    v = pltpu.VMEM
    dma = pltpu.SemaphoreType.DMA
    act = v((batch, rows, chans), BF16)

    def small(cols):
        return v((batch, 8, cols), F32)

    gout, pg, sg, eg = pl.pallas_call(
        functools.partial(fused_kernel, (zdim, share)),
        out_shape=(
            jax.ShapeDtypeStruct((batch, rows, chans), BF16),
            jax.ShapeDtypeStruct((share, chans), F32),
            jax.ShapeDtypeStruct((share, wide), F32),
            jax.ShapeDtypeStruct((share, wide), F32),
        ),
        in_specs=[vm] * 4,
        out_specs=(vm,) * 4,
        scratch_shapes=[
            v((fsdp, share, ca), BF16), v((fsdp, share, cb), BF16),
            v((chans, chans), BF16), v((chans, wide), BF16), v((chans, wide), BF16),
            act, act, act,
            v((batch, rows, chans), F32), v((rows, chans), F32), act,
            small(chans), small(wide), v((batch, GRP, chans), F32), v((GRP, chans), F32),
            small(wide), small(wide), small(chans),
            v((chans, chans + 2 * wide), F32),
            v((fsdp, share, ca), BF16), v((fsdp, share, cb), BF16),
            v((2 * zdim, share, ca), BF16), v((2 * zdim, share, cb), BF16),
            v((zdim, share, ca), BF16), v((zdim, share, cb), BF16),
            v((zdim, share, ca), BF16), v((zdim, share, cb), BF16),
            dma((2, 4, fsdp)), dma((2, fsdp)),
            dma((2, 4 * zdim)), dma((2, 4 * zdim)),
            dma((2, batch)), dma((2, batch)),
        ],
        compiler_params=pltpu.CompilerParams(collective_id=0, has_side_effects=True),
    )(by_image(inputs), by_image(cotangent), part_a, part_b)
    grads = gout[:, : positions * micro].reshape(batch, height, width, micro, chans)
    grads = grads.transpose(3, 0, 1, 2, 4)
    return grads[None], pg[None], sg[None, :, :inner], eg[:, :inner].T[None]


def suits(mesh):
    return mesh.shape["segment"] == 2 and mesh.shape["fsdp"] == 16


def solution(mesh):
    placed = (
        P(None, "fsdp", None, None, None),
        P(None, "fsdp", None, None, None),
        P("segment", "fsdp", None),
        P("segment", "fsdp", None),
        P("segment", None, "fsdp"),
    )
    return jax.shard_map(
        fused_body if suits(mesh) else body,
        mesh=mesh,
        in_specs=placed,
        out_specs=(
            P("segment", None, "fsdp", None, None, None),
            P("segment", "fsdp", None),
            P("segment", "fsdp", None),
            P("segment", None, "fsdp"),
        ),
        check_vma=False,
    )
```

```python
import functools

import jax
import jax.numpy as jnp
from jax import lax
from jax.experimental import pallas as pl
from jax.experimental.pallas import tpu as pltpu
from jax.sharding import PartitionSpec as P

HIGH = lax.Precision.HIGHEST


def shifted(block, axis, distance):
    devices = range(lax.axis_size(axis))
    route = [(i - distance, i) for i in devices if i - distance in devices]
    return lax.ppermute(block, axis, route)


def silu_slope(value):
    sig = jax.nn.sigmoid(value)
    return sig * (1.0 + value * (1.0 - sig))


def gate_values(conv, squeeze, excite):
    pooled = jnp.mean(conv, axis=1)
    u_val = jnp.dot(pooled, squeeze.astype(jnp.float32), precision=HIGH)
    gate = jax.nn.sigmoid(jnp.dot(jax.nn.silu(u_val), excite.astype(jnp.float32), precision=HIGH))
    return (pooled, u_val, gate)


def run_forward(hin, weight, squeeze, excite):
    count, chans = (hin.shape[0], hin.shape[3])
    conv = jnp.dot(hin.reshape(-1, chans), weight, preferred_element_type=jnp.float32).reshape(
        count, -1, chans
    )
    pooled, u_val, gate = gate_values(conv, squeeze, excite)
    prod = conv * gate[:, None, :]
    out = (hin.reshape(count, -1, chans).astype(jnp.float32) + jax.nn.silu(prod)).astype(
        jnp.bfloat16
    )
    return (out.reshape(hin.shape), conv, pooled, u_val)


def run_backward(grad_in, hin, weight, squeeze, excite, conv, u_val):
    count, chans = (grad_in.shape[0], grad_in.shape[3])
    positions = conv.shape[1]
    z_val = jax.nn.silu(u_val)
    gate = jax.nn.sigmoid(jnp.dot(z_val, excite.astype(jnp.float32), precision=HIGH))
    prod = conv * gate[:, None, :]
    dyf = grad_in.reshape(count, positions, chans).astype(jnp.float32)
    dprod = dyf * silu_slope(prod)
    dgate = jnp.sum(dprod * conv, axis=1)
    dv_val = dgate * gate * (1.0 - gate)
    du_val = jnp.dot(dv_val, excite.astype(jnp.float32).T, precision=HIGH) * silu_slope(u_val)
    dpooled = jnp.dot(du_val, squeeze.astype(jnp.float32).T, precision=HIGH)
    dconv = (dprod * gate[:, None, :] + dpooled[:, None, :] / positions).astype(jnp.bfloat16)
    flat_d = dconv.reshape(-1, chans)
    back = lax.dot_general(
        flat_d, weight, (((1,), (1,)), ((), ())), preferred_element_type=jnp.float32
    )
    grad_out = (dyf.reshape(-1, chans) + back).astype(jnp.bfloat16).reshape(grad_in.shape)
    w_term = lax.dot_general(
        hin.reshape(-1, chans), flat_d, (((0,), (0,)), ((), ())), preferred_element_type=jnp.float32
    )
    return (grad_out, w_term, du_val, dv_val)


def store(buffer, value, index, valid):
    old = lax.dynamic_index_in_dim(buffer, index, 0, keepdims=False)
    return lax.dynamic_update_index_in_dim(buffer, jnp.where(valid, value, old), index, 0)


def fetch(buffer, index):
    return lax.dynamic_index_in_dim(buffer, index, 0, keepdims=False)


def body(inputs, cotangent, proj, squeeze_weight, excite_weight):
    segments = lax.axis_size("segment")
    here = lax.axis_index("segment")
    micro, batch, height, width, chans = inputs.shape
    inner = squeeze_weight.shape[2]
    positions = height * width
    full_proj, full_sq, full_ex = (
        lax.all_gather(proj, "fsdp", axis=1, tiled=True),
        lax.all_gather(squeeze_weight, "fsdp", axis=1, tiled=True),
        lax.all_gather(excite_weight, "fsdp", axis=2, tiled=True),
    )
    weight, squeeze, excite = (full_proj[0], full_sq[0], full_ex[0])
    act_shape = (micro, batch, height, width, chans)

    def forward_step(tick, incoming, fbufs):
        hin_buf, conv_buf, pool_buf, u_buf = fbufs
        index = tick - here
        valid = (index >= 0) & (index < micro)
        slot = jnp.clip(index, 0, micro - 1)
        feed = jnp.where(here == 0, fetch(inputs, slot), incoming)

        def forward_active(hin):
            return run_forward(hin, weight, squeeze, excite)

        def forward_resting(hin):
            return (
                jnp.zeros(hin.shape, jnp.bfloat16),
                jnp.zeros((batch, positions, chans), jnp.float32),
                jnp.zeros((batch, chans), jnp.float32),
                jnp.zeros((batch, inner), jnp.float32),
            )

        out, conv, pooled, u_val = lax.cond(valid, forward_active, forward_resting, feed)
        fbufs = (
            store(hin_buf, feed, slot, valid),
            store(conv_buf, conv, slot, valid),
            store(pool_buf, pooled, slot, valid),
            store(u_buf, u_val, slot, valid),
        )
        sent = shifted(out, "segment", 1)
        return (sent, fbufs)

    def backward_step(tick, offset, incoming, fbufs, bbufs):
        hin_buf, conv_buf, pool_buf, u_buf = fbufs
        grad_buf, du_buf, dv_buf, w_acc = bbufs
        index = tick - offset
        valid = (index >= 0) & (index < micro)
        slot = jnp.clip(index, 0, micro - 1)
        feed = jnp.where(here == segments - 1, fetch(cotangent, slot), incoming)
        hin = fetch(hin_buf, slot)
        conv = fetch(conv_buf, slot)
        pooled = fetch(pool_buf, slot)
        u_val = fetch(u_buf, slot)

        def backward_active(grad_in):
            return run_backward(grad_in, hin, weight, squeeze, excite, conv, u_val)

        def backward_resting(grad_in):
            return (
                jnp.zeros(grad_in.shape, jnp.bfloat16),
                jnp.zeros((chans, chans), jnp.float32),
                jnp.zeros((batch, inner), jnp.float32),
                jnp.zeros((batch, chans), jnp.float32),
            )

        grad_out, w_term, du_val, dv_val = lax.cond(valid, backward_active, backward_resting, feed)
        bbufs = (
            store(grad_buf, grad_out, slot, valid),
            store(du_buf, du_val, slot, valid),
            store(dv_buf, dv_val, slot, valid),
            w_acc + w_term,
        )
        sent = shifted(grad_out, "segment", -1)
        return (sent, bbufs)

    fstart = (
        jnp.zeros(act_shape, jnp.bfloat16),
        jnp.zeros((micro, batch, positions, chans), jnp.float32),
        jnp.zeros((micro, batch, chans), jnp.float32),
        jnp.zeros((micro, batch, inner), jnp.float32),
    )
    bstart = (
        jnp.zeros(act_shape, jnp.bfloat16),
        jnp.zeros((micro, batch, inner), jnp.float32),
        jnp.zeros((micro, batch, chans), jnp.float32),
        jnp.zeros((chans, chans), jnp.float32),
    )
    empty = jnp.zeros(act_shape[1:], jnp.bfloat16)
    ticks = micro + segments - 1

    def forward_tick(tick, carry):
        return forward_step(tick, carry[0], carry[1])

    _, fbufs = lax.fori_loop(0, ticks, forward_tick, (empty, fstart))

    def backward_tick(tick, carry):
        return backward_step(tick, segments - 1 - here, carry[0], fbufs, carry[1])

    _, bbufs = lax.fori_loop(0, ticks, backward_tick, (empty, bstart))
    grad_buf, du_buf, dv_buf, w_acc = bbufs
    pool_buf, u_buf = (fbufs[2], fbufs[3])
    proj_grads = lax.psum_scatter(w_acc[None], "fsdp", scatter_dimension=1, tiled=True)
    pool_flat = pool_buf.reshape(micro * batch, chans)
    z_flat = jax.nn.silu(u_buf.reshape(micro * batch, inner))
    du_flat = du_buf.reshape(micro * batch, inner)
    dv_flat = dv_buf.reshape(micro * batch, chans)
    sq_local = jnp.dot(pool_flat.T, du_flat, precision=HIGH)
    ex_local = jnp.dot(z_flat.T, dv_flat, precision=HIGH)
    sq_total, ex_total = lax.psum((sq_local, ex_local), "fsdp")
    share = chans // lax.axis_size("fsdp")
    begin = lax.axis_index("fsdp") * share
    sq_grads = lax.dynamic_slice_in_dim(sq_total, begin, share, 0)[None]
    ex_grads = lax.dynamic_slice_in_dim(ex_total, begin, share, 1)[None]
    return (grad_buf[None], proj_grads, sq_grads, ex_grads)


MESH = pl.DeviceIdType.MESH
F32 = jnp.float32
BF16 = jnp.bfloat16
GRP = 16


def sigm(v):
    return 0.5 * jnp.tanh(0.5 * v) + 0.5


def halves(a):
    hi = a.astype(BF16).astype(F32)
    return hi, a - hi


def dot_split(a, b, transposed):
    rows = a.shape[0]
    hi, lo = halves(a)
    dims = (((1,), (1 if transposed else 0,)), ((), ()))
    out = lax.dot_general(
        jnp.concatenate([hi, lo], 0).astype(BF16), b, dims, preferred_element_type=F32
    )
    return out[:rows] + out[rows:]


def outer_split(a, b):
    fill = -a.shape[0] % GRP
    a = jnp.concatenate([a, jnp.zeros((fill, a.shape[1]), F32)], 0)
    b = jnp.concatenate([b, jnp.zeros((fill, b.shape[1]), F32)], 0)
    ah, al = halves(a)
    bh, bl = halves(b)
    left = jnp.concatenate([ah, ah, al], 0).astype(BF16)
    right = jnp.concatenate([bh, bl, bh], 0).astype(BF16)
    return lax.dot_general(left, right, (((0,), (0,)), ((), ())), preferred_element_type=F32)


def fused_kernel(
    size, x_ref, cot_ref, p_ref, s_ref, e_ref, gout_ref, pg_ref, sg_ref, eg_ref,
    a_ref, b_ref, gbuf, ga, gb, w_ref, sq_ref, ex_ref, hbuf, hnext, dybuf, conv, dpb, dconv,
    pooled, u_s, gate_s, dpool, z_s, du_s, dv_s, wg,
    sa, sb, rxa, rxb, rya, ryb, rza, rzb,
    ag_send, ag_recv, rs_send, rs_recv, relay_send, relay_recv,
):
    zdim, share = size
    chunks, positions, micro, _ = x_ref.shape
    rows = hbuf.shape[1]
    packs = rows // GRP
    chans = w_ref.shape[0]
    cut = a_ref.shape[1] - sq_ref.shape[1]
    seg = lax.axis_index("segment")
    me = lax.axis_index("fsdp")
    z, y, x = me // 4, (me // 2) % 2, me % 2
    core = (1 - seg, me)

    def place(zz, yy, xx):
        return (seg, zz * 4 + yy * 2 + xx)

    inner = s_ref.shape[1]
    a_ref[:, :cut] = p_ref[:, :cut]
    a_ref[:, cut:] = jnp.zeros((share, a_ref.shape[1] - cut), BF16)
    a_ref[:, cut : cut + inner] = s_ref[...]
    rest = chans - cut
    b_ref[:, :rest] = p_ref[:, cut:]
    b_ref[:, rest:] = jnp.zeros((share, b_ref.shape[1] - rest), BF16)
    b_ref[:, rest : rest + inner] = e_ref[...]
    for _, buf, own in ((0, ga, a_ref), (1, gb, b_ref)):
        buf[me] = own[...]

    barrier = pltpu.get_barrier_semaphore()
    pl.semaphore_signal(barrier, inc=1, device_id=core, device_id_type=MESH)
    pl.semaphore_signal(barrier, inc=1, device_id=place(z, y, 1 - x), device_id_type=MESH)
    pl.semaphore_signal(barrier, inc=1, device_id=place(z, 1 - y, x), device_id_type=MESH)
    for step in range(1, zdim):
        pl.semaphore_signal(
            barrier, inc=1, device_id=place((z + step) % zdim, y, x), device_id_type=MESH
        )
    pl.semaphore_wait(barrier, 2 + zdim)

    parts = ((0, ga, a_ref), (1, gb, b_ref))

    def flip(part, minor):
        if (part == 0) != minor:
            return z, 1 - y, x
        return z, y, 1 - x

    def ag_copy(part, buf, block, kind, target, src=None):
        return pltpu.make_async_remote_copy(
            src_ref=buf.at[block] if src is None else src,
            dst_ref=buf.at[block],
            send_sem=ag_send.at[part, kind, block],
            recv_sem=ag_recv.at[part, block],
            device_id=target,
            device_id_type=MESH,
        )

    def column(zz):
        return zz * 4 + y * 2 + x

    def first_block(part, zz):
        return zz * 4 + ((1 - y) * 2 + x if part == 0 else y * 2 + (1 - x))

    def second_block(part, zz):
        return zz * 4 + (y * 2 + (1 - x) if part == 0 else (1 - y) * 2 + x)

    def far_block(zz):
        return zz * 4 + (1 - y) * 2 + (1 - x)

    up, down = z + 1, z - 1

    def spread(part, buf, zz, src=None):
        block = column(zz)
        ag_copy(part, buf, block, 2, place(*flip(part, False)), src).start()
        ag_copy(part, buf, block, 3, place(*flip(part, True)), src).start()

    for part, buf, own in parts:
        block = column(z)

        @pl.when(up < zdim)
        def _(part=part, buf=buf, own=own, block=block):
            ag_copy(part, buf, block, 0, place(up, y, x), own).start()

        @pl.when(down >= 0)
        def _(part=part, buf=buf, own=own, block=block):
            ag_copy(part, buf, block, 1, place(down, y, x), own).start()

        spread(part, buf, z, own)
    def rows_of(q):
        return pl.ds(pl.multiple_of(q * GRP, GRP), GRP)

    def load(src, dst):
        step = GRP // micro

        def one_chunk(j, _):
            def group(q, _):
                four = [src[j, q * step + t].astype(F32) for t in range(step)]
                dst[j, rows_of(q), :] = jnp.concatenate(four, 0).astype(BF16)
                return 0

            lax.fori_loop(0, positions // step, group, 0)
            for q in range(positions // step, packs):
                four = [
                    src[j, q * step + t].astype(F32)
                    if q * step + t < positions
                    else jnp.zeros((micro, chans), F32)
                    for t in range(step)
                ]
                dst[j, q * GRP : (q + 1) * GRP, :] = jnp.concatenate(four, 0).astype(BF16)
            return 0

        lax.fori_loop(0, chunks, one_chunk, 0)

    @pl.when(seg == 0)
    def _():
        load(x_ref, hbuf)

    @pl.when(seg == 1)
    def _():
        load(cot_ref, dybuf)


    def relay_first(part, buf, zz):
        block = first_block(part, zz)
        ag_copy(part, buf, block, 3, place(*flip(part, True))).wait_recv()
        ag_copy(part, buf, block, 3, place(*flip(part, True))).start()

    for part, buf, own in parts:
        relay_first(part, buf, z)
    for dist in range(1, zdim):
        for part, buf, own in parts:

            @pl.when(z - dist >= 0)
            def _(part=part, buf=buf, dist=dist):
                block = column(z - dist)
                ag_copy(part, buf, block, 0, core).wait_recv()

                @pl.when(up < zdim)
                def _():
                    ag_copy(part, buf, block, 0, place(up, y, x)).start()

                spread(part, buf, z - dist)

            @pl.when(z + dist < zdim)
            def _(part=part, buf=buf, dist=dist):
                block = column(z + dist)
                ag_copy(part, buf, block, 1, core).wait_recv()

                @pl.when(down >= 0)
                def _():
                    ag_copy(part, buf, block, 1, place(down, y, x)).start()

                spread(part, buf, z + dist)

        for part, buf, own in parts:

            @pl.when(z - dist >= 0)
            def _(part=part, buf=buf, dist=dist):
                relay_first(part, buf, z - dist)

            @pl.when(z + dist < zdim)
            def _(part=part, buf=buf, dist=dist):
                relay_first(part, buf, z + dist)

    for part, buf, own in parts:
        for zz in range(zdim):
            ag_copy(part, buf, second_block(part, zz), 3, core).wait_recv()
            ag_copy(part, buf, far_block(zz), 3, core).wait_recv()

    def pack(k, _):
        at = pl.ds(pl.multiple_of(k * 2 * share, 2 * share), 2 * share)
        pa = jnp.concatenate([ga[2 * k].astype(F32), ga[2 * k + 1].astype(F32)], 0).astype(BF16)
        pb = jnp.concatenate([gb[2 * k].astype(F32), gb[2 * k + 1].astype(F32)], 0).astype(BF16)
        w_ref[at, :cut] = pa[:, :cut]
        sq_ref[at, :] = pa[:, cut:]
        w_ref[at, cut:] = pb[:, : chans - cut]
        ex_ref[at, :] = pb[:, chans - cut :]
        return 0

    lax.fori_loop(0, 2 * zdim, pack, 0)

    def relay(src, dst, way, j):
        return pltpu.make_async_remote_copy(
            src_ref=src.at[j],
            dst_ref=dst.at[j],
            send_sem=relay_send.at[way, j],
            recv_sem=relay_recv.at[way, j],
            device_id=core,
            device_id_type=MESH,
        )

    real = lax.broadcasted_iota(jnp.int32, (8, chans), 0) < micro

    def fold(acc):
        both = acc[:8] + acc[8:]
        return jnp.where(real, both + pltpu.roll(both, micro, 0), 0.0)

    def twice(v):
        v = jnp.where(real, v, 0.0)
        return v + pltpu.roll(v, micro, 0)

    def forward(j, _):
        @pl.when(seg == 1)
        def _():
            relay(hnext, hbuf, 0, j).wait_recv()

        conv[j] = jnp.dot(hbuf[j], w_ref[...], preferred_element_type=F32)

        def pool(q, acc):
            return acc + conv[j, rows_of(q), :]

        total = lax.fori_loop(0, packs, pool, jnp.zeros((GRP, chans), F32))
        mean = fold(total) * (1.0 / positions)
        pooled[j] = mean
        u = dot_split(mean, sq_ref[...], False)
        u_s[j] = u
        zv = u * sigm(u)
        z_s[j] = zv
        gate = twice(sigm(dot_split(zv, ex_ref[...], True)))
        gate_s[j] = jnp.concatenate([gate, gate], 0)

        @pl.when(seg == 0)
        def _():
            def emit(q, _):
                p = conv[j, rows_of(q), :] * gate_s[j]
                h = hbuf[j, rows_of(q), :].astype(F32)
                hnext[j, rows_of(q), :] = (h + p * sigm(p)).astype(BF16)
                return 0

            lax.fori_loop(0, packs, emit, 0)
            relay(hnext, hbuf, 0, j).start()

        return 0

    lax.fori_loop(0, chunks, forward, 0)

    def backward(j, _):
        @pl.when(seg == 0)
        def _():
            relay(gbuf, dybuf, 1, j).wait_recv()

        def slope(q, total):
            c = conv[j, rows_of(q), :]
            p = c * gate_s[j]
            sig = sigm(p)
            dp = dybuf[j, rows_of(q), :].astype(F32) * (sig * (1.0 + p * (1.0 - sig)))
            dpb[rows_of(q), :] = dp
            return total + dp * c

        total = lax.fori_loop(0, packs, slope, jnp.zeros((GRP, chans), F32))
        gate = gate_s[j, :8]
        dv = fold(total) * gate * (1.0 - gate)
        dv_s[j] = dv
        u = u_s[j]
        sig = sigm(u)
        du = dot_split(dv, ex_ref[...], False) * (sig * (1.0 + u * (1.0 - sig)))
        du_s[j] = du
        spread_d = twice(dot_split(du, sq_ref[...], True)) * (1.0 / positions)
        dpool[...] = jnp.concatenate([spread_d, spread_d], 0)
        spot = lax.broadcasted_iota(jnp.int32, (GRP, chans), 0)

        def finish(q, _):
            val = dpb[rows_of(q), :] * gate_s[j] + dpool[...]
            keep = spot + q * GRP < positions * micro
            dconv[j, rows_of(q), :] = jnp.where(keep, val, 0.0).astype(BF16)
            return 0

        lax.fori_loop(0, packs, finish, 0)
        back = lax.dot_general(
            dconv[j], w_ref[...], (((1,), (1,)), ((), ())), preferred_element_type=F32
        )
        gbuf[j] = (dybuf[j].astype(F32) + back).astype(BF16)

        @pl.when(seg == 1)
        def _():
            relay(gbuf, dybuf, 1, j).start()

        return 0

    lax.fori_loop(0, chunks, backward, 0)

    total_rows = chunks * rows
    flat_d = dconv[...].reshape(total_rows, chans)

    def grad_rows(k, _):
        cols = pl.ds(pl.multiple_of(k * 128, 128), 128)
        h = hbuf[:, :, cols].reshape(total_rows, 128)
        wg[pl.ds(pl.multiple_of(k * 128, 128), 128), :chans] = lax.dot_general(
            h, flat_d, (((0,), (0,)), ((), ())), preferred_element_type=F32
        )
        return 0

    lax.fori_loop(0, chans // 128, grad_rows, 0)
    wide = sq_ref.shape[1]
    small = chunks * pooled.shape[1]
    wg[:, chans : chans + wide] = outer_split(
        pooled[...].reshape(small, chans), du_s[...].reshape(small, wide)
    )
    wg[:, chans + wide :] = outer_split(
        dv_s[...].reshape(small, chans), z_s[...].reshape(small, wide)
    )

    def term(part, block):
        at = pl.ds(pl.multiple_of(block * share, 8), share)
        if part == 0:
            return wg[at, :cut], wg[at, chans : chans + wide]
        return wg[at, cut:chans], wg[at, chans + wide :]

    rs = ((0, sa, rxa, rya, rza), (1, sb, rxb, ryb, rzb))

    def joined(part, block):
        return jnp.concatenate(term(part, block), axis=1)

    def rs_copy(part, src, dst, index, target):
        return pltpu.make_async_remote_copy(
            src_ref=src,
            dst_ref=dst,
            send_sem=rs_send.at[part, index],
            recv_sem=rs_recv.at[part, index],
            device_id=target,
            device_id_type=MESH,
        )

    def z_at(k):
        return (z + 1 + k) % zdim

    def one(part, stage, r1, k, side):
        zz = z_at(k)
        block = far_block(zz) if side == 0 else second_block(part, zz)
        return block, rs_copy(
            part, stage.at[block], r1.at[2 * k + side], 2 * k + side, place(*flip(part, True))
        )

    def two(part, stage, r2, k):
        block = first_block(part, z_at(k))
        return block, rs_copy(
            part, stage.at[block], r2.at[k], 2 * zdim + k, place(*flip(part, False))
        )

    def three(part, stage, r3, k):
        block = column(z_at(k))
        return block, rs_copy(
            part, stage.at[block], r3.at[k], 3 * zdim + k, place(z_at(k), y, x)
        )

    for k in range(zdim):
        for side in range(2):
            for part, stage, r1, r2, r3 in rs:
                block, copy = one(part, stage, r1, k, side)
                stage[block] = joined(part, block).astype(BF16)
                copy.start()

    def unload(j, _):
        step = GRP // micro

        def group(q, _):
            val = gbuf[j, rows_of(q), :].astype(F32)
            for t in range(step):
                gout_ref[j, q * step + t] = val[t * micro : (t + 1) * micro].astype(BF16)
            return 0

        lax.fori_loop(0, positions // step, group, 0)
        for p in range(positions // step * step, positions):
            val = gbuf[j, p * micro // GRP * GRP : (p * micro // GRP + 1) * GRP, :].astype(F32)
            off = p * micro % GRP
            gout_ref[j, p] = val[off : off + micro].astype(BF16)
        return 0

    lax.fori_loop(0, chunks, unload, 0)

    for k in range(zdim):
        for part, stage, r1, r2, r3 in rs:
            one(part, stage, r1, k, 0)[1].wait_recv()
            block, copy = two(part, stage, r2, k)
            stage[block] = (joined(part, block) + r1[2 * k].astype(F32)).astype(BF16)
            copy.start()
    for k in range(zdim):
        for part, stage, r1, r2, r3 in rs:
            one(part, stage, r1, k, 1)[1].wait_recv()
            two(part, stage, r2, k)[1].wait_recv()
            if k < zdim - 1:
                block, copy = three(part, stage, r3, k)
                value = joined(part, block) + r1[2 * k + 1].astype(F32) + r2[k].astype(F32)
                stage[block] = value.astype(BF16)
                copy.start()
    last = zdim - 1
    for part, stage, r1, r2, r3 in rs:
        value = joined(part, me) + r1[2 * last + 1].astype(F32) + r2[last].astype(F32)
        for k in range(zdim - 1):
            three(part, stage, r3, k)[1].wait_recv()
            value = value + r3[k].astype(F32)
        if part == 0:
            pg_ref[:, :cut] = value[:, :cut]
            sg_ref[...] = value[:, cut : cut + inner]
        else:
            pg_ref[:, cut:] = value[:, : chans - cut]
            eg_ref[...] = value[:, rest : rest + inner]

    for part, stage, r1, r2, r3 in rs:
        for k in range(zdim):
            one(part, stage, r1, k, 0)[1].wait_send()
            one(part, stage, r1, k, 1)[1].wait_send()
            two(part, stage, r2, k)[1].wait_send()
            if k < zdim - 1:
                three(part, stage, r3, k)[1].wait_send()
    for part, buf, own in parts:
        for zz in range(zdim):
            ag_copy(part, buf, column(zz), 2, core).wait_send()
            ag_copy(part, buf, column(zz), 3, core).wait_send()
            ag_copy(part, buf, first_block(part, zz), 3, core).wait_send()

            @pl.when((zz <= z) & (up < zdim))
            def _(part=part, buf=buf, zz=zz):
                ag_copy(part, buf, column(zz), 0, core).wait_send()

            @pl.when((zz >= z) & (down >= 0))
            def _(part=part, buf=buf, zz=zz):
                ag_copy(part, buf, column(zz), 1, core).wait_send()

    for j in range(chunks):

        @pl.when(seg == 0)
        def _(j=j):
            relay(hnext, hbuf, 0, j).wait_send()

        @pl.when(seg == 1)
        def _(j=j):
            relay(gbuf, dybuf, 1, j).wait_send()


def fused_body(inputs, cotangent, proj, squeeze_weight, excite_weight):
    fsdp = lax.axis_size("fsdp")
    micro, batch, height, width, chans = inputs.shape
    share, inner = squeeze_weight.shape[1:]
    zdim = fsdp // 4
    positions = height * width
    rows = -(-positions * micro // GRP) * GRP
    wide = -(-inner // 128) * 128
    cut = (chans // 128 + 1) // 2 * 128

    def by_image(arr):
        return arr.transpose(1, 2, 3, 0, 4).reshape(batch, positions, micro, chans)

    ca, cb = cut + wide, chans - cut + wide
    vm = pl.BlockSpec(memory_space=pltpu.VMEM)
    v = pltpu.VMEM
    dma = pltpu.SemaphoreType.DMA
    act = v((batch, rows, chans), BF16)

    def small(cols):
        return v((batch, 8, cols), F32)

    gout, pg, sg, eg = pl.pallas_call(
        functools.partial(fused_kernel, (zdim, share)),
        out_shape=(
            jax.ShapeDtypeStruct((batch, positions, micro, chans), BF16),
            jax.ShapeDtypeStruct((share, chans), F32),
            jax.ShapeDtypeStruct((share, inner), F32),
            jax.ShapeDtypeStruct((share, inner), F32),
        ),
        in_specs=[vm] * 5,
        out_specs=(vm,) * 4,
        scratch_shapes=[
            v((share, ca), BF16), v((share, cb), BF16), act,
            v((fsdp, share, ca), BF16), v((fsdp, share, cb), BF16),
            v((chans, chans), BF16), v((chans, wide), BF16), v((chans, wide), BF16),
            act, act, act,
            v((batch, rows, chans), F32), v((rows, chans), F32), act,
            small(chans), small(wide), v((batch, GRP, chans), F32), v((GRP, chans), F32),
            small(wide), small(wide), small(chans),
            v((chans, chans + 2 * wide), F32),
            v((fsdp, share, ca), BF16), v((fsdp, share, cb), BF16),
            v((2 * zdim, share, ca), BF16), v((2 * zdim, share, cb), BF16),
            v((zdim, share, ca), BF16), v((zdim, share, cb), BF16),
            v((zdim, share, ca), BF16), v((zdim, share, cb), BF16),
            dma((2, 4, fsdp)), dma((2, fsdp)),
            dma((2, 4 * zdim)), dma((2, 4 * zdim)),
            dma((2, batch)), dma((2, batch)),
        ],
        compiler_params=pltpu.CompilerParams(collective_id=0, has_side_effects=True),
    )(by_image(inputs), by_image(cotangent), proj[0], squeeze_weight[0], excite_weight[0].T)
    grads = gout.reshape(batch, height, width, micro, chans)
    grads = grads.transpose(3, 0, 1, 2, 4)
    return grads[None], pg[None], sg[None], eg.T[None]


def suits(mesh):
    return mesh.shape["segment"] == 2 and mesh.shape["fsdp"] == 16


def solution(mesh):
    placed = (
        P(None, "fsdp", None, None, None),
        P(None, "fsdp", None, None, None),
        P("segment", "fsdp", None),
        P("segment", "fsdp", None),
        P("segment", None, "fsdp"),
    )
    return jax.shard_map(
        fused_body if suits(mesh) else body,
        mesh=mesh,
        in_specs=placed,
        out_specs=(
            P("segment", None, "fsdp", None, None, None),
            P("segment", "fsdp", None),
            P("segment", "fsdp", None),
            P("segment", None, "fsdp"),
        ),
        check_vma=False,
    )
```

```python
import functools

import jax
import jax.numpy as jnp
from jax import lax
from jax.experimental import pallas as pl
from jax.experimental.pallas import tpu as pltpu
from jax.sharding import PartitionSpec as P

HIGH = lax.Precision.HIGHEST


def shifted(block, axis, distance):
    devices = range(lax.axis_size(axis))
    route = [(i - distance, i) for i in devices if i - distance in devices]
    return lax.ppermute(block, axis, route)


def silu_slope(value):
    sig = jax.nn.sigmoid(value)
    return sig * (1.0 + value * (1.0 - sig))


def gate_values(conv, squeeze, excite):
    pooled = jnp.mean(conv, axis=1)
    u_val = jnp.dot(pooled, squeeze.astype(jnp.float32), precision=HIGH)
    gate = jax.nn.sigmoid(jnp.dot(jax.nn.silu(u_val), excite.astype(jnp.float32), precision=HIGH))
    return (pooled, u_val, gate)


def run_forward(hin, weight, squeeze, excite):
    count, chans = (hin.shape[0], hin.shape[3])
    conv = jnp.dot(hin.reshape(-1, chans), weight, preferred_element_type=jnp.float32).reshape(
        count, -1, chans
    )
    pooled, u_val, gate = gate_values(conv, squeeze, excite)
    prod = conv * gate[:, None, :]
    out = (hin.reshape(count, -1, chans).astype(jnp.float32) + jax.nn.silu(prod)).astype(
        jnp.bfloat16
    )
    return (out.reshape(hin.shape), conv, pooled, u_val)


def run_backward(grad_in, hin, weight, squeeze, excite, conv, u_val):
    count, chans = (grad_in.shape[0], grad_in.shape[3])
    positions = conv.shape[1]
    z_val = jax.nn.silu(u_val)
    gate = jax.nn.sigmoid(jnp.dot(z_val, excite.astype(jnp.float32), precision=HIGH))
    prod = conv * gate[:, None, :]
    dyf = grad_in.reshape(count, positions, chans).astype(jnp.float32)
    dprod = dyf * silu_slope(prod)
    dgate = jnp.sum(dprod * conv, axis=1)
    dv_val = dgate * gate * (1.0 - gate)
    du_val = jnp.dot(dv_val, excite.astype(jnp.float32).T, precision=HIGH) * silu_slope(u_val)
    dpooled = jnp.dot(du_val, squeeze.astype(jnp.float32).T, precision=HIGH)
    dconv = (dprod * gate[:, None, :] + dpooled[:, None, :] / positions).astype(jnp.bfloat16)
    flat_d = dconv.reshape(-1, chans)
    back = lax.dot_general(
        flat_d, weight, (((1,), (1,)), ((), ())), preferred_element_type=jnp.float32
    )
    grad_out = (dyf.reshape(-1, chans) + back).astype(jnp.bfloat16).reshape(grad_in.shape)
    w_term = lax.dot_general(
        hin.reshape(-1, chans), flat_d, (((0,), (0,)), ((), ())), preferred_element_type=jnp.float32
    )
    return (grad_out, w_term, du_val, dv_val)


def store(buffer, value, index, valid):
    old = lax.dynamic_index_in_dim(buffer, index, 0, keepdims=False)
    return lax.dynamic_update_index_in_dim(buffer, jnp.where(valid, value, old), index, 0)


def fetch(buffer, index):
    return lax.dynamic_index_in_dim(buffer, index, 0, keepdims=False)


def body(inputs, cotangent, proj, squeeze_weight, excite_weight):
    segments = lax.axis_size("segment")
    here = lax.axis_index("segment")
    micro, batch, height, width, chans = inputs.shape
    inner = squeeze_weight.shape[2]
    positions = height * width
    full_proj, full_sq, full_ex = (
        lax.all_gather(proj, "fsdp", axis=1, tiled=True),
        lax.all_gather(squeeze_weight, "fsdp", axis=1, tiled=True),
        lax.all_gather(excite_weight, "fsdp", axis=2, tiled=True),
    )
    weight, squeeze, excite = (full_proj[0], full_sq[0], full_ex[0])
    act_shape = (micro, batch, height, width, chans)

    def forward_step(tick, incoming, fbufs):
        hin_buf, conv_buf, pool_buf, u_buf = fbufs
        index = tick - here
        valid = (index >= 0) & (index < micro)
        slot = jnp.clip(index, 0, micro - 1)
        feed = jnp.where(here == 0, fetch(inputs, slot), incoming)

        def forward_active(hin):
            return run_forward(hin, weight, squeeze, excite)

        def forward_resting(hin):
            return (
                jnp.zeros(hin.shape, jnp.bfloat16),
                jnp.zeros((batch, positions, chans), jnp.float32),
                jnp.zeros((batch, chans), jnp.float32),
                jnp.zeros((batch, inner), jnp.float32),
            )

        out, conv, pooled, u_val = lax.cond(valid, forward_active, forward_resting, feed)
        fbufs = (
            store(hin_buf, feed, slot, valid),
            store(conv_buf, conv, slot, valid),
            store(pool_buf, pooled, slot, valid),
            store(u_buf, u_val, slot, valid),
        )
        sent = shifted(out, "segment", 1)
        return (sent, fbufs)

    def backward_step(tick, offset, incoming, fbufs, bbufs):
        hin_buf, conv_buf, pool_buf, u_buf = fbufs
        grad_buf, du_buf, dv_buf, w_acc = bbufs
        index = tick - offset
        valid = (index >= 0) & (index < micro)
        slot = jnp.clip(index, 0, micro - 1)
        feed = jnp.where(here == segments - 1, fetch(cotangent, slot), incoming)
        hin = fetch(hin_buf, slot)
        conv = fetch(conv_buf, slot)
        pooled = fetch(pool_buf, slot)
        u_val = fetch(u_buf, slot)

        def backward_active(grad_in):
            return run_backward(grad_in, hin, weight, squeeze, excite, conv, u_val)

        def backward_resting(grad_in):
            return (
                jnp.zeros(grad_in.shape, jnp.bfloat16),
                jnp.zeros((chans, chans), jnp.float32),
                jnp.zeros((batch, inner), jnp.float32),
                jnp.zeros((batch, chans), jnp.float32),
            )

        grad_out, w_term, du_val, dv_val = lax.cond(valid, backward_active, backward_resting, feed)
        bbufs = (
            store(grad_buf, grad_out, slot, valid),
            store(du_buf, du_val, slot, valid),
            store(dv_buf, dv_val, slot, valid),
            w_acc + w_term,
        )
        sent = shifted(grad_out, "segment", -1)
        return (sent, bbufs)

    fstart = (
        jnp.zeros(act_shape, jnp.bfloat16),
        jnp.zeros((micro, batch, positions, chans), jnp.float32),
        jnp.zeros((micro, batch, chans), jnp.float32),
        jnp.zeros((micro, batch, inner), jnp.float32),
    )
    bstart = (
        jnp.zeros(act_shape, jnp.bfloat16),
        jnp.zeros((micro, batch, inner), jnp.float32),
        jnp.zeros((micro, batch, chans), jnp.float32),
        jnp.zeros((chans, chans), jnp.float32),
    )
    empty = jnp.zeros(act_shape[1:], jnp.bfloat16)
    ticks = micro + segments - 1

    def forward_tick(tick, carry):
        return forward_step(tick, carry[0], carry[1])

    _, fbufs = lax.fori_loop(0, ticks, forward_tick, (empty, fstart))

    def backward_tick(tick, carry):
        return backward_step(tick, segments - 1 - here, carry[0], fbufs, carry[1])

    _, bbufs = lax.fori_loop(0, ticks, backward_tick, (empty, bstart))
    grad_buf, du_buf, dv_buf, w_acc = bbufs
    pool_buf, u_buf = (fbufs[2], fbufs[3])
    proj_grads = lax.psum_scatter(w_acc[None], "fsdp", scatter_dimension=1, tiled=True)
    pool_flat = pool_buf.reshape(micro * batch, chans)
    z_flat = jax.nn.silu(u_buf.reshape(micro * batch, inner))
    du_flat = du_buf.reshape(micro * batch, inner)
    dv_flat = dv_buf.reshape(micro * batch, chans)
    sq_local = jnp.dot(pool_flat.T, du_flat, precision=HIGH)
    ex_local = jnp.dot(z_flat.T, dv_flat, precision=HIGH)
    sq_total, ex_total = lax.psum((sq_local, ex_local), "fsdp")
    share = chans // lax.axis_size("fsdp")
    begin = lax.axis_index("fsdp") * share
    sq_grads = lax.dynamic_slice_in_dim(sq_total, begin, share, 0)[None]
    ex_grads = lax.dynamic_slice_in_dim(ex_total, begin, share, 1)[None]
    return (grad_buf[None], proj_grads, sq_grads, ex_grads)


MESH = pl.DeviceIdType.MESH
F32 = jnp.float32
BF16 = jnp.bfloat16
GRP = 16


def sigm(v):
    return 0.5 * jnp.tanh(0.5 * v) + 0.5


def halves(a):
    hi = a.astype(BF16).astype(F32)
    return hi, a - hi


def dot_split(a, b, transposed):
    rows = a.shape[0]
    hi, lo = halves(a)
    dims = (((1,), (1 if transposed else 0,)), ((), ()))
    out = lax.dot_general(
        jnp.concatenate([hi, lo], 0).astype(BF16), b, dims, preferred_element_type=F32
    )
    return out[:rows] + out[rows:]


def outer_split(a, b):
    fill = -a.shape[0] % GRP
    a = jnp.concatenate([a, jnp.zeros((fill, a.shape[1]), F32)], 0)
    b = jnp.concatenate([b, jnp.zeros((fill, b.shape[1]), F32)], 0)
    ah, al = halves(a)
    bh, bl = halves(b)
    left = jnp.concatenate([ah, ah, al], 0).astype(BF16)
    right = jnp.concatenate([bh, bl, bh], 0).astype(BF16)
    return lax.dot_general(left, right, (((0,), (0,)), ((), ())), preferred_element_type=F32)


def fused_kernel(
    size, x_ref, cot_ref, p_ref, s_ref, e_ref, gout_ref, wg_ref,
    a_ref, b_ref, gbuf, ga, gb, w_ref, sq_ref, ex_ref, hbuf, hnext, dybuf, conv, dpb, dconv,
    pooled, u_s, gate_s, dpool, z_s, du_s, dv_s, wg,
    sa, sb, rxa, rxb, rya, ryb, rza, rzb,
    ag_send, ag_recv, rs_send, rs_recv, relay_send, relay_recv,
):
    zdim, share = size
    chunks, positions, micro, _ = x_ref.shape
    rows = hbuf.shape[1]
    packs = rows // GRP
    chans = w_ref.shape[0]
    cut = a_ref.shape[1] - sq_ref.shape[1]
    seg = lax.axis_index("segment")
    me = lax.axis_index("fsdp")
    z, y, x = me // 4, (me // 2) % 2, me % 2
    core = (1 - seg, me)

    def place(zz, yy, xx):
        return (seg, zz * 4 + yy * 2 + xx)

    inner = s_ref.shape[1]
    a_ref[:, :cut] = p_ref[:, :cut]
    a_ref[:, cut:] = jnp.zeros((share, a_ref.shape[1] - cut), BF16)
    a_ref[:, cut : cut + inner] = s_ref[...]
    rest = chans - cut
    b_ref[:, :rest] = p_ref[:, cut:]
    b_ref[:, rest:] = jnp.zeros((share, b_ref.shape[1] - rest), BF16)
    b_ref[:, rest : rest + inner] = e_ref[...]
    for _, buf, own in ((0, ga, a_ref), (1, gb, b_ref)):
        buf[me] = own[...]

    barrier = pltpu.get_barrier_semaphore()
    pl.semaphore_signal(barrier, inc=1, device_id=core, device_id_type=MESH)
    pl.semaphore_signal(barrier, inc=1, device_id=place(z, y, 1 - x), device_id_type=MESH)
    pl.semaphore_signal(barrier, inc=1, device_id=place(z, 1 - y, x), device_id_type=MESH)
    for step in range(1, zdim):
        pl.semaphore_signal(
            barrier, inc=1, device_id=place((z + step) % zdim, y, x), device_id_type=MESH
        )
    pl.semaphore_wait(barrier, 2 + zdim)

    parts = ((0, ga, a_ref), (1, gb, b_ref))

    def flip(part, minor):
        if (part == 0) != minor:
            return z, 1 - y, x
        return z, y, 1 - x

    def ag_copy(part, buf, block, kind, target, src=None):
        return pltpu.make_async_remote_copy(
            src_ref=buf.at[block] if src is None else src,
            dst_ref=buf.at[block],
            send_sem=ag_send.at[part, kind, block],
            recv_sem=ag_recv.at[part, block],
            device_id=target,
            device_id_type=MESH,
        )

    def column(zz):
        return zz * 4 + y * 2 + x

    def first_block(part, zz):
        return zz * 4 + ((1 - y) * 2 + x if part == 0 else y * 2 + (1 - x))

    def second_block(part, zz):
        return zz * 4 + (y * 2 + (1 - x) if part == 0 else (1 - y) * 2 + x)

    def far_block(zz):
        return zz * 4 + (1 - y) * 2 + (1 - x)

    up, down = z + 1, z - 1

    def spread(part, buf, zz, src=None):
        block = column(zz)
        ag_copy(part, buf, block, 2, place(*flip(part, False)), src).start()
        ag_copy(part, buf, block, 3, place(*flip(part, True)), src).start()

    for part, buf, own in parts:
        block = column(z)

        @pl.when(up < zdim)
        def _(part=part, buf=buf, own=own, block=block):
            ag_copy(part, buf, block, 0, place(up, y, x), own).start()

        @pl.when(down >= 0)
        def _(part=part, buf=buf, own=own, block=block):
            ag_copy(part, buf, block, 1, place(down, y, x), own).start()

        spread(part, buf, z, own)
    def rows_of(q):
        return pl.ds(pl.multiple_of(q * GRP, GRP), GRP)

    def load(src, dst):
        step = GRP // micro

        def one_chunk(j, _):
            def group(q, _):
                four = [src[j, q * step + t].astype(F32) for t in range(step)]
                dst[j, rows_of(q), :] = jnp.concatenate(four, 0).astype(BF16)
                return 0

            lax.fori_loop(0, positions // step, group, 0)
            for q in range(positions // step, packs):
                four = [
                    src[j, q * step + t].astype(F32)
                    if q * step + t < positions
                    else jnp.zeros((micro, chans), F32)
                    for t in range(step)
                ]
                dst[j, q * GRP : (q + 1) * GRP, :] = jnp.concatenate(four, 0).astype(BF16)
            return 0

        lax.fori_loop(0, chunks, one_chunk, 0)

    @pl.when(seg == 0)
    def _():
        load(x_ref, hbuf)

    @pl.when(seg == 1)
    def _():
        load(cot_ref, dybuf)


    def relay_first(part, buf, zz):
        block = first_block(part, zz)
        ag_copy(part, buf, block, 3, place(*flip(part, True))).wait_recv()
        ag_copy(part, buf, block, 3, place(*flip(part, True))).start()

    for part, buf, own in parts:
        relay_first(part, buf, z)
    for dist in range(1, zdim):
        for part, buf, own in parts:

            @pl.when(z - dist >= 0)
            def _(part=part, buf=buf, dist=dist):
                block = column(z - dist)
                ag_copy(part, buf, block, 0, core).wait_recv()

                @pl.when(up < zdim)
                def _():
                    ag_copy(part, buf, block, 0, place(up, y, x)).start()

                spread(part, buf, z - dist)

            @pl.when(z + dist < zdim)
            def _(part=part, buf=buf, dist=dist):
                block = column(z + dist)
                ag_copy(part, buf, block, 1, core).wait_recv()

                @pl.when(down >= 0)
                def _():
                    ag_copy(part, buf, block, 1, place(down, y, x)).start()

                spread(part, buf, z + dist)

        for part, buf, own in parts:

            @pl.when(z - dist >= 0)
            def _(part=part, buf=buf, dist=dist):
                relay_first(part, buf, z - dist)

            @pl.when(z + dist < zdim)
            def _(part=part, buf=buf, dist=dist):
                relay_first(part, buf, z + dist)

    for part, buf, own in parts:
        for zz in range(zdim):
            ag_copy(part, buf, second_block(part, zz), 3, core).wait_recv()
            ag_copy(part, buf, far_block(zz), 3, core).wait_recv()

    def pack(k, _):
        at = pl.ds(pl.multiple_of(k * 2 * share, 2 * share), 2 * share)
        pa = jnp.concatenate([ga[2 * k].astype(F32), ga[2 * k + 1].astype(F32)], 0).astype(BF16)
        pb = jnp.concatenate([gb[2 * k].astype(F32), gb[2 * k + 1].astype(F32)], 0).astype(BF16)
        w_ref[at, :cut] = pa[:, :cut]
        sq_ref[at, :] = pa[:, cut:]
        w_ref[at, cut:] = pb[:, : chans - cut]
        ex_ref[at, :] = pb[:, chans - cut :]
        return 0

    lax.fori_loop(0, 2 * zdim, pack, 0)

    def relay(src, dst, way, j):
        return pltpu.make_async_remote_copy(
            src_ref=src.at[j],
            dst_ref=dst.at[j],
            send_sem=relay_send.at[way, j],
            recv_sem=relay_recv.at[way, j],
            device_id=core,
            device_id_type=MESH,
        )

    real = lax.broadcasted_iota(jnp.int32, (8, chans), 0) < micro

    def fold(acc):
        both = acc[:8] + acc[8:]
        return jnp.where(real, both + pltpu.roll(both, micro, 0), 0.0)

    def twice(v):
        v = jnp.where(real, v, 0.0)
        return v + pltpu.roll(v, micro, 0)

    def forward(j, _):
        @pl.when(seg == 1)
        def _():
            relay(hnext, hbuf, 0, j).wait_recv()

        conv[j] = jnp.dot(hbuf[j], w_ref[...], preferred_element_type=F32)

        def pool(q, acc):
            return acc + conv[j, rows_of(q), :]

        total = lax.fori_loop(0, packs, pool, jnp.zeros((GRP, chans), F32))
        mean = fold(total) * (1.0 / positions)
        pooled[j] = mean
        u = dot_split(mean, sq_ref[...], False)
        u_s[j] = u
        zv = u * sigm(u)
        z_s[j] = zv
        gate = twice(sigm(dot_split(zv, ex_ref[...], True)))
        gate_s[j] = jnp.concatenate([gate, gate], 0)

        @pl.when(seg == 0)
        def _():
            def emit(q, _):
                p = conv[j, rows_of(q), :] * gate_s[j]
                h = hbuf[j, rows_of(q), :].astype(F32)
                hnext[j, rows_of(q), :] = (h + p * sigm(p)).astype(BF16)
                return 0

            lax.fori_loop(0, packs, emit, 0)
            relay(hnext, hbuf, 0, j).start()

        return 0

    lax.fori_loop(0, chunks, forward, 0)

    def backward(j, _):
        @pl.when(seg == 0)
        def _():
            relay(gbuf, dybuf, 1, j).wait_recv()

        def slope(q, total):
            c = conv[j, rows_of(q), :]
            p = c * gate_s[j]
            sig = sigm(p)
            dp = dybuf[j, rows_of(q), :].astype(F32) * (sig * (1.0 + p * (1.0 - sig)))
            dpb[rows_of(q), :] = dp
            return total + dp * c

        total = lax.fori_loop(0, packs, slope, jnp.zeros((GRP, chans), F32))
        gate = gate_s[j, :8]
        dv = fold(total) * gate * (1.0 - gate)
        dv_s[j] = dv
        u = u_s[j]
        sig = sigm(u)
        du = dot_split(dv, ex_ref[...], False) * (sig * (1.0 + u * (1.0 - sig)))
        du_s[j] = du
        spread_d = twice(dot_split(du, sq_ref[...], True)) * (1.0 / positions)
        dpool[...] = jnp.concatenate([spread_d, spread_d], 0)
        spot = lax.broadcasted_iota(jnp.int32, (GRP, chans), 0)

        def finish(q, _):
            val = dpb[rows_of(q), :] * gate_s[j] + dpool[...]
            keep = spot + q * GRP < positions * micro
            dconv[j, rows_of(q), :] = jnp.where(keep, val, 0.0).astype(BF16)
            return 0

        lax.fori_loop(0, packs, finish, 0)
        back = lax.dot_general(
            dconv[j], w_ref[...], (((1,), (1,)), ((), ())), preferred_element_type=F32
        )
        gbuf[j] = (dybuf[j].astype(F32) + back).astype(BF16)

        @pl.when(seg == 1)
        def _():
            relay(gbuf, dybuf, 1, j).start()

        return 0

    lax.fori_loop(0, chunks, backward, 0)

    total_rows = chunks * rows
    flat_d = dconv[...].reshape(total_rows, chans)

    def grad_rows(k, _):
        cols = pl.ds(pl.multiple_of(k * 128, 128), 128)
        h = hbuf[:, :, cols].reshape(total_rows, 128)
        wg[pl.ds(pl.multiple_of(k * 128, 128), 128), :chans] = lax.dot_general(
            h, flat_d, (((0,), (0,)), ((), ())), preferred_element_type=F32
        )
        return 0

    lax.fori_loop(0, chans // 128, grad_rows, 0)
    wide = sq_ref.shape[1]
    small = chunks * pooled.shape[1]
    wg[:, chans : chans + wide] = outer_split(
        pooled[...].reshape(small, chans), du_s[...].reshape(small, wide)
    )
    wg[:, chans + wide :] = outer_split(
        dv_s[...].reshape(small, chans), z_s[...].reshape(small, wide)
    )

    def term(part, block):
        at = pl.ds(pl.multiple_of(block * share, 8), share)
        if part == 0:
            return wg[at, :cut], wg[at, chans : chans + wide]
        return wg[at, cut:chans], wg[at, chans + wide :]

    rs = ((0, sa, rxa, rya, rza), (1, sb, rxb, ryb, rzb))

    def joined(part, block):
        return jnp.concatenate(term(part, block), axis=1)

    def rs_copy(part, src, dst, index, target):
        return pltpu.make_async_remote_copy(
            src_ref=src,
            dst_ref=dst,
            send_sem=rs_send.at[part, index],
            recv_sem=rs_recv.at[part, index],
            device_id=target,
            device_id_type=MESH,
        )

    def z_at(k):
        return (z + 1 + k) % zdim

    def one(part, stage, r1, k, side):
        zz = z_at(k)
        block = far_block(zz) if side == 0 else second_block(part, zz)
        return block, rs_copy(
            part, stage.at[block], r1.at[2 * k + side], 2 * k + side, place(*flip(part, True))
        )

    def two(part, stage, r2, k):
        block = first_block(part, z_at(k))
        return block, rs_copy(
            part, stage.at[block], r2.at[k], 2 * zdim + k, place(*flip(part, False))
        )

    def three(part, stage, r3, k):
        block = column(z_at(k))
        return block, rs_copy(
            part, stage.at[block], r3.at[k], 3 * zdim + k, place(z_at(k), y, x)
        )

    for k in range(zdim):
        for side in range(2):
            for part, stage, r1, r2, r3 in rs:
                block, copy = one(part, stage, r1, k, side)
                stage[block] = joined(part, block).astype(BF16)
                copy.start()

    def unload(j, _):
        step = GRP // micro

        def group(q, _):
            val = gbuf[j, rows_of(q), :].astype(F32)
            for t in range(step):
                gout_ref[j, q * step + t] = val[t * micro : (t + 1) * micro].astype(BF16)
            return 0

        lax.fori_loop(0, positions // step, group, 0)
        for p in range(positions // step * step, positions):
            val = gbuf[j, p * micro // GRP * GRP : (p * micro // GRP + 1) * GRP, :].astype(F32)
            off = p * micro % GRP
            gout_ref[j, p] = val[off : off + micro].astype(BF16)
        return 0

    lax.fori_loop(0, chunks, unload, 0)

    for k in range(zdim):
        for part, stage, r1, r2, r3 in rs:
            one(part, stage, r1, k, 0)[1].wait_recv()
            block, copy = two(part, stage, r2, k)
            stage[block] = (joined(part, block) + r1[2 * k].astype(F32)).astype(BF16)
            copy.start()
    for k in range(zdim):
        for part, stage, r1, r2, r3 in rs:
            one(part, stage, r1, k, 1)[1].wait_recv()
            two(part, stage, r2, k)[1].wait_recv()
            if k < zdim - 1:
                block, copy = three(part, stage, r3, k)
                value = joined(part, block) + r1[2 * k + 1].astype(F32) + r2[k].astype(F32)
                stage[block] = value.astype(BF16)
                copy.start()
    last = zdim - 1
    for part, stage, r1, r2, r3 in rs:
        value = joined(part, me) + r1[2 * last + 1].astype(F32) + r2[last].astype(F32)
        for k in range(zdim - 1):
            three(part, stage, r3, k)[1].wait_recv()
            value = value + r3[k].astype(F32)
        if part == 0:
            wg_ref[:, :cut] = value[:, :cut]
            wg_ref[:, chans : chans + wide] = value[:, cut:]
        else:
            wg_ref[:, cut:chans] = value[:, :rest]
            wg_ref[:, chans + wide :] = value[:, rest:]

    for part, stage, r1, r2, r3 in rs:
        for k in range(zdim):
            one(part, stage, r1, k, 0)[1].wait_send()
            one(part, stage, r1, k, 1)[1].wait_send()
            two(part, stage, r2, k)[1].wait_send()
            if k < zdim - 1:
                three(part, stage, r3, k)[1].wait_send()
    for part, buf, own in parts:
        for zz in range(zdim):
            ag_copy(part, buf, column(zz), 2, core).wait_send()
            ag_copy(part, buf, column(zz), 3, core).wait_send()
            ag_copy(part, buf, first_block(part, zz), 3, core).wait_send()

            @pl.when((zz <= z) & (up < zdim))
            def _(part=part, buf=buf, zz=zz):
                ag_copy(part, buf, column(zz), 0, core).wait_send()

            @pl.when((zz >= z) & (down >= 0))
            def _(part=part, buf=buf, zz=zz):
                ag_copy(part, buf, column(zz), 1, core).wait_send()

    for j in range(chunks):

        @pl.when(seg == 0)
        def _(j=j):
            relay(hnext, hbuf, 0, j).wait_send()

        @pl.when(seg == 1)
        def _(j=j):
            relay(gbuf, dybuf, 1, j).wait_send()


def fused_body(inputs, cotangent, proj, squeeze_weight, excite_weight):
    fsdp = lax.axis_size("fsdp")
    micro, batch, height, width, chans = inputs.shape
    share, inner = squeeze_weight.shape[1:]
    zdim = fsdp // 4
    positions = height * width
    rows = -(-positions * micro // GRP) * GRP
    wide = -(-inner // 128) * 128
    cut = (chans // 128 + 1) // 2 * 128

    def by_image(arr):
        return arr.transpose(1, 2, 3, 0, 4).reshape(batch, positions, micro, chans)

    ca, cb = cut + wide, chans - cut + wide
    vm = pl.BlockSpec(memory_space=pltpu.VMEM)
    v = pltpu.VMEM
    dma = pltpu.SemaphoreType.DMA
    act = v((batch, rows, chans), BF16)

    def small(cols):
        return v((batch, 8, cols), F32)

    gout, terms = pl.pallas_call(
        functools.partial(fused_kernel, (zdim, share)),
        out_shape=(
            jax.ShapeDtypeStruct((batch, positions, micro, chans), BF16),
            jax.ShapeDtypeStruct((share, chans + 2 * wide), F32),
        ),
        in_specs=[vm] * 5,
        out_specs=(vm,) * 2,
        scratch_shapes=[
            v((share, ca), BF16), v((share, cb), BF16), act,
            v((fsdp, share, ca), BF16), v((fsdp, share, cb), BF16),
            v((chans, chans), BF16), v((chans, wide), BF16), v((chans, wide), BF16),
            act, act, act,
            v((batch, rows, chans), F32), v((rows, chans), F32), act,
            small(chans), small(wide), v((batch, GRP, chans), F32), v((GRP, chans), F32),
            small(wide), small(wide), small(chans),
            v((chans, chans + 2 * wide), F32),
            v((fsdp, share, ca), BF16), v((fsdp, share, cb), BF16),
            v((2 * zdim, share, ca), BF16), v((2 * zdim, share, cb), BF16),
            v((zdim, share, ca), BF16), v((zdim, share, cb), BF16),
            v((zdim, share, ca), BF16), v((zdim, share, cb), BF16),
            dma((2, 4, fsdp)), dma((2, fsdp)),
            dma((2, 4 * zdim)), dma((2, 4 * zdim)),
            dma((2, batch)), dma((2, batch)),
        ],
        compiler_params=pltpu.CompilerParams(collective_id=0, has_side_effects=True),
    )(by_image(inputs), by_image(cotangent), proj[0], squeeze_weight[0], excite_weight[0].T)
    grads = gout.reshape(batch, height, width, micro, chans)
    grads = grads.transpose(3, 0, 1, 2, 4)
    at = chans + wide
    sg, eg = terms[:, chans : chans + inner], terms[:, at : at + inner]
    return grads[None], terms[None, :, :chans], sg[None], eg.T[None]


def suits(mesh):
    return mesh.shape["segment"] == 2 and mesh.shape["fsdp"] == 16


def solution(mesh):
    placed = (
        P(None, "fsdp", None, None, None),
        P(None, "fsdp", None, None, None),
        P("segment", "fsdp", None),
        P("segment", "fsdp", None),
        P("segment", None, "fsdp"),
    )
    return jax.shard_map(
        fused_body if suits(mesh) else body,
        mesh=mesh,
        in_specs=placed,
        out_specs=(
            P("segment", None, "fsdp", None, None, None),
            P("segment", "fsdp", None),
            P("segment", "fsdp", None),
            P("segment", None, "fsdp"),
        ),
        check_vma=False,
    )
```
